512 devices in a mesh: row: 32 (over y, x, core), col: 16 (over z).
Axes of the slice: x: 4, y: 4, z: 16, core: 2. Of those that a mesh axis runs over, the one named last changes fastest.
Arguments:
- slab_blocks: bfloat16 [49152, 8192], P('row', 'col'), may hold values from -6 to 6
- slot_tiles: int32 [192, 16], P('row', 'col'), may hold values from 0 to 7, as said below
- live_counts: int32 [32, 16], P('row', 'col'), may hold values from 1 to 6, as said below
- first_prior: float32 [16384, 256], P(('row', 'col'))
- second_prior: float32 [16384, 256], P(('col', 'row')), may hold values from -6 to 6
- first_test: bfloat16 [16384, 256], P('row'), may hold values from -0.046875 to 0.046875
- second_test: bfloat16 [16384, 256], P('col'), may hold values from -0.046875 to 0.046875
- third_test: bfloat16 [2, 256], replicated, may hold values from -4 to 4
- core_first: bfloat16 [512, 16384], P(None, 'row'), may hold values from -0.046875 to 0.046875
- core_second: bfloat16 [16384, 512], P('col'), may hold values from -0.046875 to 0.046875
- core_third: bfloat16 [512, 2], replicated, may hold values from -4 to 4
Outputs:
- first_sketch: float32 [16384, 256], P(('row', 'col'))
- second_sketch: float32 [16384, 256], P(('col', 'row'))
- third_sketch: float32 [2, 256], replicated
- core_update: float32 [512, 512, 512], P('row', 'col')
- first_basis: float32 [16384, 256], P(('row', 'col'))
The draws below stay inside these ranges and needn't reach their ends.
Inputs may be any that keep to these rules, and one draw needn't show every extreme that they name: `slot_tiles`: within one region pair the first 6 slots name distinct block positions. `live_counts`: some region pair has all 6 slots live.
All inputs are finite; a program needn't handle non-finite values.
Results may differ from the reference program's by a relative error of at most 0.0029.
Values sent between devices are 32-bit elements; how exact they have to be, the bound alone decides.
A program may use at most 64 MiB of HBM per device.

```python
import math
import jax
import jax.numpy as jnp
from jax import lax

TILE = 256
FACTOR = 256
CORE = 512
DEPTH = 2
TILE_ROWS = 2
TILE_COLS = 4
SLOTS = 6
MODE_ONE = 16384
MODE_TWO = 16384
N_ROW = 32
N_COL = 16


def draw_slot_tiles(key, part):
    key_list = jax.random.split(key, N_ROW * N_COL)
    orders = jax.vmap(lambda single: jax.random.permutation(single, TILE_ROWS * TILE_COLS))(key_list)
    chosen = orders[:, :SLOTS].reshape(N_ROW, N_COL, SLOTS)
    return jnp.transpose(chosen, (0, 2, 1)).reshape(N_ROW * SLOTS, N_COL).astype(jnp.int32)


def draw_live_counts(key, part):
    levels = jax.random.randint(key, (N_ROW * N_COL,), 0, SLOTS)
    counts_flat = 1 + levels * levels // SLOTS
    fullest = jax.random.randint(jax.random.fold_in(key, 7), (), 0, N_ROW * N_COL)
    counts_flat = jnp.where(jnp.arange(N_ROW * N_COL) == fullest, SLOTS, counts_flat)
    return counts_flat.reshape(N_ROW, N_COL).astype(jnp.int32)


def draw_first_prior(key, part):
    key_rows, key_cols, key_vals = jax.random.split(key, 3)
    row_scale = jnp.exp(jax.random.uniform(key_rows, (MODE_ONE, 1), jnp.float32, 0.0, math.log(10.0)))
    col_scale = jnp.exp(jax.random.uniform(key_cols, (1, FACTOR), jnp.float32, 0.0, math.log(10.0)))
    values = jax.random.normal(key_vals, (MODE_ONE, FACTOR), jnp.float32)
    return (0.3 * row_scale * col_scale * values).astype(jnp.float32)


def block_levels(stream_key, extent, cuts, low, high):
    level, own = 1.0, jax.random.fold_in(stream_key, 6)
    for axis_at, blocks in cuts:
        draws = jnp.exp(jax.random.uniform(jax.random.fold_in(own, axis_at), (blocks,), jnp.float32, low / len(cuts), high / len(cuts)))
        level = level * jnp.repeat(draws, extent[axis_at] // blocks).reshape([-1 if axis == axis_at else 1 for axis in range(len(extent))])
    return level


def noise(rng, shape, width, bound, shards=(), held_as=jnp.bfloat16):
    array = width * jax.random.normal(rng, shape, jnp.float32)
    if shards:
        array = array * block_levels(rng, shape, shards, -0.22, 0.18)
    return jnp.clip(array, -bound, bound).astype(held_as)


def setup_inputs(seed: int = 0) -> dict:
    keys = jax.random.split(jax.random.key(seed), 12)
    slab_blocks = noise(keys[0], (N_ROW * SLOTS * TILE, N_COL * DEPTH * TILE), 1.0, 6.0, ((0, 32), (1, 16)))
    slot_tiles = draw_slot_tiles(jax.random.fold_in(keys[11], 71), 0)
    live_counts = draw_live_counts(jax.random.fold_in(keys[11], 71), 0)
    first_prior = draw_first_prior(jax.random.fold_in(keys[11], 71), 0)
    second_prior = noise(keys[4], (MODE_TWO, FACTOR), 1.0, 6.0, ((0, 512),), jnp.float32)
    first_test = noise(keys[5], (MODE_ONE, FACTOR), MODE_ONE ** -0.5, 0.046875, ((0, 32),))
    second_test = noise(keys[6], (MODE_TWO, FACTOR), MODE_TWO ** -0.5, 0.046875, ((0, 16),))
    third_test = noise(keys[7], (DEPTH, FACTOR), DEPTH ** -0.5, 4.0)
    core_first = noise(keys[8], (CORE, MODE_ONE), MODE_ONE ** -0.5, 0.046875, ((1, 32),))
    core_second = noise(keys[9], (MODE_TWO, CORE), MODE_TWO ** -0.5, 0.046875, ((0, 16),))
    core_third = noise(keys[10], (CORE, DEPTH), DEPTH ** -0.5, 4.0)
    return {"slab_blocks": slab_blocks, "slot_tiles": slot_tiles, "live_counts": live_counts, "first_prior": first_prior, "second_prior": second_prior, "first_test": first_test, "second_test": second_test, "third_test": third_test, "core_first": core_first, "core_second": core_second, "core_third": core_third}


def add_rows(target, update, start):
    current = lax.dynamic_slice_in_dim(target, start, update.shape[0], 0)
    return lax.dynamic_update_slice_in_dim(target, current + update, start, 0)

def reference(slab_blocks, slot_tiles, live_counts, first_prior, second_prior, first_test, second_test, third_test, core_first, core_second, core_third):
    row_span = TILE_ROWS * TILE
    col_span = TILE_COLS * TILE
    mixed_one = (third_test.astype(jnp.float32)[:, None, :] * second_test.astype(jnp.float32)[None, :, :]).astype(jnp.bfloat16)
    mixed_two = (first_test.astype(jnp.float32)[:, None, :] * third_test.astype(jnp.float32)[None, :, :]).astype(jnp.bfloat16)

    def device_step(running, device_index):
        first_all, second_all, third_all, core_all = running
        grid_row = (device_index // N_COL).astype(jnp.int32)
        grid_col = (device_index % N_COL).astype(jnp.int32)
        row_base = (grid_row * row_span).astype(jnp.int32)
        col_base = (grid_col * col_span).astype(jnp.int32)
        blocks_here = lax.dynamic_slice(slab_blocks, ((grid_row * (SLOTS * TILE)).astype(jnp.int32), (grid_col * (DEPTH * TILE)).astype(jnp.int32)), (SLOTS * TILE, DEPTH * TILE))
        places = lax.dynamic_slice(slot_tiles, ((grid_row * SLOTS).astype(jnp.int32), grid_col), (SLOTS, 1))
        live_slots = lax.dynamic_slice(live_counts, (grid_row, grid_col), (1, 1))[0, 0].astype(jnp.int32)

        def slot_step(slot_index, inside):
            first_acc, second_acc, third_acc, region = inside
            block_data = lax.dynamic_slice_in_dim(blocks_here, (slot_index * TILE).astype(jnp.int32), TILE, 0)
            flat_block = block_data.reshape(TILE * DEPTH, TILE)
            tile_place = places[slot_index, 0].astype(jnp.int32)
            local_row = (tile_place // TILE_COLS * TILE).astype(jnp.int32)
            row_start = (row_base + local_row).astype(jnp.int32)
            col_start = (col_base + tile_place % TILE_COLS * TILE).astype(jnp.int32)
            left_mix = lax.dynamic_slice_in_dim(mixed_one, col_start, TILE, 1).reshape(DEPTH * TILE, FACTOR)
            right_mix = lax.dynamic_slice_in_dim(mixed_two, row_start, TILE, 0).reshape(TILE * DEPTH, FACTOR)
            first_acc = add_rows(first_acc, jnp.dot(block_data.astype(jnp.float32), left_mix.astype(jnp.float32), preferred_element_type=jnp.float32), row_start)
            second_acc = add_rows(second_acc, jnp.dot(flat_block.T.astype(jnp.float32), right_mix.astype(jnp.float32), preferred_element_type=jnp.float32), col_start)
            across = jnp.dot(flat_block.astype(jnp.float32), lax.dynamic_slice_in_dim(second_test, col_start, TILE, 0).astype(jnp.float32), preferred_element_type=jnp.float32)
            weights = lax.dynamic_slice_in_dim(first_test, row_start, TILE, 0).astype(jnp.float32)
            third_acc = third_acc + jnp.sum(across.reshape(TILE, DEPTH, FACTOR) * weights[:, None, :], axis=0)
            projected = jnp.dot(flat_block.astype(jnp.float32), lax.dynamic_slice_in_dim(core_second, col_start, TILE, 0).astype(jnp.float32), preferred_element_type=jnp.float32)
            region = add_rows(region, projected.reshape(TILE, DEPTH * CORE), local_row)
            return (first_acc, second_acc, third_acc, region)
        region_start = jnp.zeros((row_span, DEPTH * CORE), jnp.float32)
        first_all, second_all, third_all, region = lax.fori_loop(0, live_slots, slot_step, (first_all, second_all, third_all, region_start))
        core_first_here = lax.dynamic_slice_in_dim(core_first, row_base, row_span, 1)
        core_all = core_all + jnp.dot(core_first_here.astype(jnp.float32), region.astype(jnp.bfloat16).astype(jnp.float32), preferred_element_type=jnp.float32)
        return ((first_all, second_all, third_all, core_all), None)
    start_state = (jnp.zeros((MODE_ONE, FACTOR), jnp.float32), jnp.zeros((MODE_TWO, FACTOR), jnp.float32), jnp.zeros((DEPTH, FACTOR), jnp.float32), jnp.zeros((CORE, DEPTH * CORE), jnp.float32))
    final_state, unused = lax.scan(device_step, start_state, jnp.arange(N_ROW * N_COL, dtype=jnp.int32))
    first_all, second_all, third_sketch, core_all = final_state
    first_sketch = first_prior + first_all
    second_sketch = second_prior + second_all
    core_rows = core_all.reshape(CORE, DEPTH, CORE)
    core_update = jnp.einsum('plq,sl->pqs', core_rows, core_third.astype(jnp.float32), precision=lax.Precision.HIGHEST)
    gram_total = jnp.dot(first_sketch.T.astype(jnp.float32), first_sketch.astype(jnp.float32), precision=lax.Precision.HIGHEST, preferred_element_type=jnp.float32)
    chol_lower = jnp.linalg.cholesky(gram_total)
    first_basis = jax.scipy.linalg.solve_triangular(chol_lower, first_sketch.T, lower=True).T
    return (first_sketch, second_sketch, third_sketch, core_update, first_basis)
```

```python
import functools

import jax
import jax.numpy as jnp
from jax import lax
from jax.experimental import pallas as pl
from jax.experimental.pallas import tpu as pltpu
from jax.sharding import PartitionSpec as P

F32 = jnp.float32
BF16 = jnp.bfloat16
HIGHEST = lax.Precision.HIGHEST


def in_blocks(array, dim, count):
    lengths = array.shape
    tiles = array.reshape(*lengths[:dim], count, lengths[dim] // count, *lengths[dim + 1 :])
    return jnp.moveaxis(tiles, dim, 0)


def sum_at_owner(array, axis, dim):
    tiles = in_blocks(array, dim, lax.axis_size(axis))
    arrived = lax.all_to_all(tiles, axis, split_axis=0, concat_axis=0, tiled=True)
    return arrived.sum(axis=0)


def dot(a, b, dims=((1,), (0,)), precision=None):
    return lax.dot_general(a, b, (dims, ((), ())), precision=precision, preferred_element_type=F32)


def local_kernel(tiles_ref, live_ref, slab, first_t, second_t, third_t, core_f, core_s, first_o, second_o, third_o, core_o, dense, region):
    tile = slab.shape[1] // 2
    slots = slab.shape[0] // tile
    rows, cols = first_t.shape[0], second_t.shape[0]
    tile_cols = cols // tile
    live = live_ref[0, 0]
    for tr in range(rows // tile):
        for tc in range(tile_cols):
            slot, valid = jnp.int32(0), jnp.int32(0)
            for s in range(slots):
                here = jnp.logical_and(tiles_ref[s, 0] == tr * tile_cols + tc, s < live)
                slot = jnp.where(here, s, slot)
                valid = jnp.where(here, 1, valid)
            block = slab[pl.ds(pl.multiple_of(slot * tile, tile), tile), :]
            block = block * valid.astype(F32).astype(BF16)
            dense[tr * tile : (tr + 1) * tile, tc * tile : (tc + 1) * tile] = block[:, :tile]
            dense[tr * tile : (tr + 1) * tile, cols + tc * tile : cols + (tc + 1) * tile] = block[:, tile:]
    third = third_t[...].astype(F32)
    second = second_t[...]
    first_f = first_t[...].astype(F32)
    first_sum, second_sum = None, None
    width = core_s.shape[1]
    for level in range(2):
        part = dense[:, level * cols : (level + 1) * cols]
        mixed_one = (third[level : level + 1, :] * second.astype(F32)).astype(BF16)
        mixed_two = (first_f * third[level : level + 1, :]).astype(BF16)
        one = dot(part, mixed_one)
        two = dot(part, mixed_two, ((0,), (0,)))
        first_sum = one if level == 0 else first_sum + one
        second_sum = two if level == 0 else second_sum + two
        across = dot(part, second)
        third_o[level : level + 1, :] = jnp.sum(across * first_f, axis=0, keepdims=True)
        region[:, level * width : (level + 1) * width] = dot(part, core_s[...]).astype(BF16)
    first_o[...] = first_sum
    second_o[...] = second_sum
    core_o[...] = dot(core_f[...], region[...])


def local_products(slot_tiles, live_counts, slab, first_t, second_t, third_t, core_f, core_s):
    smem = pl.BlockSpec(memory_space=pltpu.SMEM)
    vmem = pl.BlockSpec(memory_space=pltpu.VMEM)
    rows, cols, factor, width = first_t.shape[0], second_t.shape[0], first_t.shape[1], core_s.shape[1]
    shapes = ((rows, factor), (cols, factor), (2, factor), (core_f.shape[0], 2 * width))
    return pl.pallas_call(
        local_kernel,
        out_shape=[jax.ShapeDtypeStruct(s, F32) for s in shapes],
        in_specs=[smem, smem] + [vmem] * 6,
        out_specs=[vmem] * 4,
        scratch_shapes=[pltpu.VMEM((rows, 2 * cols), BF16), pltpu.VMEM((rows, 2 * width), BF16)],
        compiler_params=pltpu.CompilerParams(vmem_limit_bytes=40 * 2**20),
    )(slot_tiles, live_counts, slab, first_t, second_t, third_t, core_f, core_s)


def eliminate(work, size, wide=32, group=8):
    row_at = lax.broadcasted_iota(jnp.int32, (wide, 128), 0)
    row_full = lax.broadcasted_iota(jnp.int32, (wide, size), 0)
    lane_full = lax.broadcasted_iota(jnp.int32, (wide, size), 1)
    for start in range(0, size, wide):
        panel = work[start : start + wide, :]
        inverse_pivots = jnp.zeros((wide, 128), F32)
        for base in range(0, wide, group):
            columns = [
                jnp.broadcast_to(panel[:, start + base + k : start + base + k + 1], (wide, 128)) for k in range(group)
            ]
            for k in range(group):
                row = base + k
                inverse = 1.0 / jnp.broadcast_to(columns[k][row : row + 1, :], (wide, 128))
                inverse_pivots = jnp.where(row_at == row, inverse, inverse_pivots)
                factor = jnp.where(row_at > row, columns[k] * inverse, 0.0)
                for later in range(k + 1, group):
                    columns[later] = columns[later] - factor * columns[later][row : row + 1, :]
                here = lane_full == start + row
                pivot_row = jnp.where(here[row : row + 1, :], 1.0, panel[row : row + 1, :])
                kept = jnp.where(jnp.logical_and(here, row_full > row), 0.0, panel)
                panel = kept - jnp.concatenate([factor] * (size // 128), axis=1) * pivot_row
        work[start : start + wide, :] = panel
        rest = size - start - wide
        if rest:
            inside = jnp.logical_and(lane_full >= start, lane_full < start + wide)
            unit = jnp.where(lane_full == start + row_full, 1.0, panel)
            unit = jnp.where(jnp.logical_and(inside, lane_full > start + row_full), 0.0, unit)
            scaled = jnp.where(inside, unit, 0.0) * jnp.concatenate([inverse_pivots] * (size // 128), axis=1)
            step = dot(scaled, unit, ((0,), (0,)), HIGHEST)
            below = work[start + wide :, :]
            lane_rest = lax.broadcasted_iota(jnp.int32, (rest, size), 1)
            inside_rest = jnp.logical_and(lane_rest >= start, lane_rest < start + wide)
            change = dot(jnp.where(inside_rest, below, 0.0), step, precision=HIGHEST)
            work[start + wide :, :] = jnp.where(inside_rest, 0.0, below) - change


def basis_kernel(gram, sketch, basis, work):
    size = gram.shape[0]
    work[...] = gram[...]
    eliminate(work, size)
    row = lax.broadcasted_iota(jnp.int32, (size, size), 0)
    lane = lax.broadcasted_iota(jnp.int32, (size, size), 1)
    whole = work[...]
    pivots = jnp.sum(jnp.where(row == lane, whole, 0.0), axis=1, keepdims=True)
    inverse = jnp.where(lane < row, whole, jnp.where(lane == row, 1.0, 0.0)) * lax.rsqrt(pivots)
    basis[...] = dot(sketch[...], inverse, ((1,), (1,)), HIGHEST)


def basis_of(gram, sketch):
    vmem = pl.BlockSpec(memory_space=pltpu.VMEM)
    return pl.pallas_call(
        basis_kernel,
        out_shape=jax.ShapeDtypeStruct(sketch.shape, F32),
        in_specs=[vmem, vmem],
        out_specs=vmem,
        scratch_shapes=[pltpu.VMEM(gram.shape, F32)],
    )(gram, sketch)


def body(slab, slot_tiles, live_counts, first_prior, second_prior, first_t, second_t, third_t, core_f, core_s, core_t):
    factor, width = first_t.shape[1], core_s.shape[1]
    first_part, second_part, third_part, core_rows = local_products(
        slot_tiles, live_counts, slab, first_t, second_t, third_t, core_f, core_s
    )
    first_sketch = first_prior + sum_at_owner(first_part, "col", 0)
    second_sketch = second_prior + sum_at_owner(second_part, "row", 0)
    sectioned = sum_at_owner(core_rows.reshape(-1, 2, width), "row", 0)
    core_share = sum_at_owner(sectioned, "col", 2)
    core_update = jnp.einsum("plq,sl->pqs", core_share, core_t.astype(F32), precision=HIGHEST)
    gram_part = dot(first_sketch, first_sketch, ((0,), (0,)), HIGHEST)
    combined = lax.psum(jnp.concatenate([gram_part, third_part], axis=0), ("row", "col"))
    first_basis = basis_of(combined[:factor], first_sketch)
    return (first_sketch, second_sketch, combined[factor:], core_update, first_basis)


def solution(mesh):
    both, swapped = P(("row", "col"), None), P(("col", "row"), None)
    return jax.shard_map(
        body,
        mesh=mesh,
        in_specs=(
            P("row", "col"), P("row", "col"), P("row", "col"), both, swapped,
            P("row", None), P("col", None), P(), P(None, "row"), P("col", None), P(),
        ),
        out_specs=(both, swapped, P(), P("row", "col", None), both),
        check_vma=False,
    )
```

```python
import functools

import jax
import jax.numpy as jnp
from jax import lax
from jax.experimental import pallas as pl
from jax.experimental.pallas import tpu as pltpu
from jax.sharding import PartitionSpec as P

F32 = jnp.float32
BF16 = jnp.bfloat16
HIGHEST = lax.Precision.HIGHEST


def dot(a, b, dims=((1,), (0,)), precision=None):
    return lax.dot_general(a, b, (dims, ((), ())), precision=precision, preferred_element_type=F32)


MESH = pl.DeviceIdType.MESH
SIDE = 4


def ring_order(count):
    return sorted(range(1, count), key=lambda step: -min(step, count - step))


class Sender:
    def __init__(self, send_sems, recv_sems):
        self.send_sems, self.recv_sems, self.copies = send_sems, recv_sems, []

    def __call__(self, source, target, device):
        at = len(self.copies)
        copy = pltpu.make_async_remote_copy(
            src_ref=source, dst_ref=target, send_sem=self.send_sems.at[at], recv_sem=self.recv_sems.at[at],
            device_id=device, device_id_type=MESH,
        )
        copy.start()
        self.copies.append(copy)
        return copy


def arrive(copies):
    for copy in copies:
        copy.wait_recv()


def sums_kernel(
    tiles_ref, live_ref, slab_h, first_h, second_h, third_h, core_f_h, core_s_h, first_prior, second_prior,
    first_o, second_o, third_o, gram_o, share_o,
    slab, first_t, second_t, third_t, core_f, core_s, dense, region,
    first_v, second_v, core_v, third_v, down, up, second_c, core_c, third_c,
    second_1, core_1, second_2, core_2, third_xy, third_z,
    gram_v, gram_c, gram_xy, gram_own, gram_z, gram_done, pieces, pieces_in,
    load_sems, send_sems, recv_sems,
):
    tile = slab.shape[1] // 2
    slots = slab.shape[0] // tile
    rows, cols = first_t.shape[0], second_t.shape[0]
    tile_cols = cols // tile
    width = core_s.shape[1]
    factor = first_t.shape[1]
    row, z = lax.axis_index("row"), lax.axis_index("col")
    rings = lax.axis_size("col")
    core = row % 2
    chip = row // 2
    y, x = chip // SIDE, chip % SIDE
    chips = SIDE * SIDE

    loads = [
        pltpu.make_async_copy(source, target, load_sems.at[i])
        for i, (source, target) in enumerate(
            ((slab_h, slab), (third_h, third_t), (second_h, second_t), (first_h, first_t), (core_s_h, core_s), (core_f_h, core_f))
        )
    ]
    for load in loads:
        load.start()

    def at_chip(dy, dx):
        return ((((y + dy) % SIDE) * SIDE + (x + dx) % SIDE) * 2 + core, z)

    def at_ring(step):
        return (row, (z + step + rings) % rings)

    partner = (chip * 2 + 1 - core, z)
    offsets = sorted(
        [(dy, dx) for dy in range(SIDE) for dx in range(SIDE) if dy or dx],
        key=lambda o: -(min(o[0], SIDE - o[0]) + min(o[1], SIDE - o[1])),
    )
    barrier = pltpu.get_barrier_semaphore()
    others = [partner] + [at_chip(*o) for o in offsets] + [at_ring(s) for s in range(1, rings)]
    for device in others:
        pl.semaphore_signal(barrier, inc=1, device_id=device, device_id_type=MESH)

    send = Sender(send_sems, recv_sems)
    live = live_ref[0, 0]
    places = (rows // tile) * tile_cols
    weights = [
        [jnp.logical_and(tiles_ref[s, 0] == t, s < live).astype(jnp.int32).astype(F32).astype(BF16) for s in range(slots)]
        for t in range(places)
    ]
    loads[0].wait()

    def place_rows(i, carry):
        blocks = [slab[pl.ds(pl.multiple_of(s * tile + i * 16, 16), 16), :] for s in range(slots)]
        for t in range(places):
            block = blocks[0] * weights[t][0]
            for s in range(1, slots):
                block = block + blocks[s] * weights[t][s]
            tr, tc = t // tile_cols, t % tile_cols
            at = pl.ds(pl.multiple_of(tr * tile + i * 16, 16), 16)
            dense[at, tc * tile : (tc + 1) * tile] = block[:, :tile]
            dense[at, cols + tc * tile : cols + (tc + 1) * tile] = block[:, tile:]
        return carry

    lax.fori_loop(0, tile // 16, place_rows, 0)
    loads[1].wait()
    loads[2].wait()
    third = third_t[...].astype(F32)
    halves = [dense.at[:, level * cols : (level + 1) * cols] for level in range(2)]
    first_sum = None
    for level in range(2):
        mixed = (third[level : level + 1, :] * second_t[...].astype(F32)).astype(BF16)
        term = dot(halves[level][...], mixed)
        first_sum = term if level == 0 else first_sum + term
    span = rows // rings
    first_v[...] = first_sum.reshape(rings, span, factor)
    pl.semaphore_wait(barrier, len(others))

    half = rings // 2
    down_copies = [send(first_v.at[(z + half) % rings], down.at[0], at_ring(-1))]
    up_copies = [send(first_v.at[(z + half - 1) % rings], up.at[0], at_ring(1))]

    def first_step(step):
        down_copies[step - 1].wait_recv()
        down[step - 1] = down[step - 1] + first_v[(z + half + step) % rings]
        down_copies.append(send(down.at[step - 1], down.at[step], at_ring(-1)))
        if step < half - 1:
            up_copies[step - 1].wait_recv()
            up[step - 1] = up[step - 1] + first_v[(z + half - 1 - step + rings) % rings]
            up_copies.append(send(up.at[step - 1], up.at[step], at_ring(1)))

    loads[3].wait()
    second_sum = None
    for level in range(2):
        mixed = (first_t[...].astype(F32) * third[level : level + 1, :]).astype(BF16)
        term = dot(halves[level][...], mixed, ((0,), (0,)))
        second_sum = term if level == 0 else second_sum + term
    second_v[...] = second_sum.reshape(second_v.shape)
    second_swap = send(second_v.at[:, :, 1 - core], second_c, partner)
    for level in range(2):
        across = dot(halves[level][...], second_t[...])
        third_v[0:1, level * factor : (level + 1) * factor] = jnp.sum(across * first_t[...].astype(F32), axis=0, keepdims=True)
    third_swap = send(third_v, third_c.at[core], partner)
    first_step(1)
    loads[4].wait()
    for level in range(2):
        region[:, level * width : (level + 1) * width] = dot(halves[level][...], core_s[...]).astype(BF16)
    loads[5].wait()
    core_v[...] = dot(core_f[...], region[...]).reshape(core_v.shape)
    core_swap = send(core_v.at[:, :, 1 - core], core_c, partner)
    first_step(2)

    def start_xy(total, landing):
        rows_half = total.shape[2] // 2
        copies = []
        for step in (2, 1, 3):
            to_x, to_y = (x + step) % SIDE, (y + step) % SIDE
            copies.append(send(total.at[:, to_x, 0:rows_half], landing.at[0, step - 1], at_chip(0, step)))
            copies.append(send(total.at[to_y, :, rows_half:], landing.at[1, step - 1], at_chip(step, 0)))
        return copies

    def middle_xy(total, landing, last):
        rows_half = total.shape[2] // 2
        landing[0, 0] = total[:, x, 0:rows_half] + landing[0, 0] + landing[0, 1] + landing[0, 2]
        landing[1, 0] = total[y, :, rows_half:] + landing[1, 0] + landing[1, 1] + landing[1, 2]
        copies = []
        for step in (2, 1, 3):
            to_x, to_y = (x + step) % SIDE, (y + step) % SIDE
            copies.append(send(landing.at[0, 0, to_y], last.at[0, step - 1], at_chip(step, 0)))
            copies.append(send(landing.at[1, 0, to_x], last.at[1, step - 1], at_chip(0, step)))
        return copies

    second_swap.wait_recv()
    second_c[...] = second_c[...] + second_v[:, :, core]
    second_stage = start_xy(second_c, second_1)
    third_swap.wait_recv()
    third_c[core] = third_v[...]
    third_xy[chip] = third_c[0] + third_c[1]
    third_stage = [send(third_xy.at[chip], third_xy.at[chip], at_chip(*o)) for o in offsets]
    first_step(3)
    core_swap.wait_recv()
    core_c[...] = core_c[...] + core_v[:, :, core]
    core_stage = start_xy(core_c, core_1)
    first_step(4)
    arrive(second_stage)
    second_last = middle_xy(second_c, second_1, second_2)
    arrive(third_stage)
    third_sum = third_xy[0]
    for i in range(1, chips):
        third_sum = third_sum + third_xy[i]
    third_z[z] = third_sum
    third_last = [send(third_z.at[z], third_z.at[z], at_ring(s)) for s in ring_order(rings)]
    first_step(5)
    arrive(core_stage)
    core_last = middle_xy(core_c, core_1, core_2)
    first_step(6)
    arrive(second_last)
    rows_half = second_c.shape[2] // 2
    second_o[0:rows_half, :] = second_prior[0:rows_half, :] + (second_1[0, 0, y] + second_2[0, 0] + second_2[0, 1] + second_2[0, 2])
    second_o[rows_half:, :] = second_prior[rows_half:, :] + (second_1[1, 0, x] + second_2[1, 0] + second_2[1, 1] + second_2[1, 2])
    first_step(7)
    up_copies[-1].wait_recv()
    sketch = first_prior[...] + first_v[z] + up[half - 2]
    down_copies[-1].wait_recv()
    sketch = sketch + down[half - 1]
    first_o[...] = sketch

    gram_v[...] = dot(sketch, sketch, ((0,), (0,)), HIGHEST).reshape(gram_v.shape)
    gram_swap = send(gram_v.at[1 - core], gram_c, partner)

    arrive(core_last)
    rows_half = core_c.shape[2] // 2
    lane = lax.broadcasted_iota(jnp.int32, (rows_half, 128), 1) // 32
    sums = [
        core_1[0, 0, y] + core_2[0, 0] + core_2[0, 1] + core_2[0, 2],
        core_1[1, 0, x] + core_2[1, 0] + core_2[1, 1] + core_2[1, 2],
    ]
    for group in range(width // 128):
        parts = [sums[k // 2][:, (k % 2) * width + group * 128 : (k % 2) * width + (group + 1) * 128] for k in range(4)]
        for m in range(4):
            piece = None
            for k in range(4):
                shift = (k - m) * 32 % 128
                moved = pltpu.roll(parts[k], shift, 1) if shift else parts[k]
                piece = moved if k == 0 else jnp.where(lane == k, moved, piece)
            pieces[group * 4 + m] = piece

    gram_swap.wait_recv()
    gram_c[...] = gram_c[...] + gram_v[core]
    gram_stage = [
        send(gram_c.at[((y + dy) % SIDE) * SIDE + (x + dx) % SIDE], gram_xy.at[dy * SIDE + dx], at_chip(dy, dx)) for dy, dx in offsets
    ]
    arrive(third_last)
    third_sum = third_z[0]
    for i in range(1, rings):
        third_sum = third_sum + third_z[i]
    third_o[...] = third_sum
    arrive(gram_stage)
    total = gram_c[chip]
    for i in range(1, chips):
        total = total + gram_xy[i]
    gram_own[...] = total
    gram_ring = [send(gram_own, gram_z.at[s], at_ring(s)) for s in ring_order(rings)]
    arrive(gram_ring)
    for i in range(1, rings):
        total = total + gram_z[i]
    gram_done[core, chip] = total
    gram_spread = [send(gram_done.at[core, chip], gram_done.at[core, chip], at_chip(*o)) for o in offsets]
    share_stage = [send(pieces.at[(z + s) % rings], pieces_in.at[s], at_ring(s)) for s in ring_order(rings)]
    arrive(gram_spread)
    gram_back = send(gram_done.at[core], gram_done.at[core], partner)
    arrive(share_stage)
    share = pieces[z]
    for i in range(1, rings):
        share = share + pieces_in[i]
    share_o[...] = share
    gram_back.wait_recv()
    gram_o[...] = gram_done[...].reshape(gram_o.shape)
    for copy in send.copies:
        copy.wait_send()


def all_sums(slot_tiles, live_counts, slab, first_t, second_t, third_t, core_f, core_s, first_prior, second_prior):
    smem, vmem, hbm = (pl.BlockSpec(memory_space=m) for m in (pltpu.SMEM, pltpu.VMEM, pl.ANY))
    rows, cols, factor, width = first_t.shape[0], second_t.shape[0], first_t.shape[1], core_s.shape[1]
    rings = lax.axis_size("col")
    chips = SIDE * SIDE
    owned, high = second_prior.shape[0], core_f.shape[0] // lax.axis_size("row")
    span = rows // rings
    half = rings // 2

    def f32(*shape):
        return pltpu.VMEM(shape, F32)

    scratch = [
        *(pltpu.VMEM(a.shape, BF16) for a in (slab, first_t, second_t, third_t, core_f, core_s)),
        pltpu.VMEM((rows, 2 * cols), BF16), pltpu.VMEM((rows, 2 * width), BF16),
        f32(rings, span, factor), f32(SIDE, SIDE, 2, owned, factor), f32(SIDE, SIDE, 2, high, 2 * width), f32(1, 2 * factor),
        f32(half, span, factor), f32(half - 1, span, factor),
        f32(SIDE, SIDE, owned, factor), f32(SIDE, SIDE, high, 2 * width), f32(2, 1, 2 * factor),
        f32(2, SIDE - 1, SIDE, owned // 2, factor), f32(2, SIDE - 1, SIDE, high // 2, 2 * width),
        f32(2, SIDE - 1, owned // 2, factor), f32(2, SIDE - 1, high // 2, 2 * width),
        f32(chips, 1, 2 * factor), f32(rings, 1, 2 * factor),
        f32(2, chips, 8, factor), f32(chips, 8, factor), f32(chips, 8, factor), f32(8, factor), f32(rings, 8, factor),
        f32(2, chips, 8, factor), f32(rings, 8, 128), f32(rings, 8, 128),
        pltpu.SemaphoreType.DMA((6,)), pltpu.SemaphoreType.DMA((160,)), pltpu.SemaphoreType.DMA((160,)),
    ]
    shapes = (first_prior.shape, second_prior.shape, (1, 2 * factor), (factor, factor), (8, 128))
    return pl.pallas_call(
        sums_kernel,
        out_shape=[jax.ShapeDtypeStruct(s, F32) for s in shapes],
        in_specs=[smem, smem] + [hbm] * 6 + [vmem] * 2,
        out_specs=[vmem] * 5,
        scratch_shapes=scratch,
        compiler_params=pltpu.CompilerParams(collective_id=0, has_side_effects=True, vmem_limit_bytes=60 * 2**20),
    )(slot_tiles, live_counts, slab, first_t, second_t, third_t, core_f, core_s, first_prior, second_prior)


def eliminate(work, size, wide=32, group=8):
    row_at = lax.broadcasted_iota(jnp.int32, (wide, 128), 0)
    row_full = lax.broadcasted_iota(jnp.int32, (wide, size), 0)
    lane_full = lax.broadcasted_iota(jnp.int32, (wide, size), 1)
    for start in range(0, size, wide):
        panel = work[start : start + wide, :]
        inverse_pivots = jnp.zeros((wide, 128), F32)
        for base in range(0, wide, group):
            columns = [
                jnp.broadcast_to(panel[:, start + base + k : start + base + k + 1], (wide, 128)) for k in range(group)
            ]
            for k in range(group):
                row = base + k
                inverse = 1.0 / jnp.broadcast_to(columns[k][row : row + 1, :], (wide, 128))
                inverse_pivots = jnp.where(row_at == row, inverse, inverse_pivots)
                factor = jnp.where(row_at > row, columns[k] * inverse, 0.0)
                for later in range(k + 1, group):
                    columns[later] = columns[later] - factor * columns[later][row : row + 1, :]
                here = lane_full == start + row
                pivot_row = jnp.where(here[row : row + 1, :], 1.0, panel[row : row + 1, :])
                kept = jnp.where(jnp.logical_and(here, row_full > row), 0.0, panel)
                panel = kept - jnp.concatenate([factor] * (size // 128), axis=1) * pivot_row
        work[start : start + wide, :] = panel
        rest = size - start - wide
        if rest:
            inside = jnp.logical_and(lane_full >= start, lane_full < start + wide)
            unit = jnp.where(lane_full == start + row_full, 1.0, panel)
            unit = jnp.where(jnp.logical_and(inside, lane_full > start + row_full), 0.0, unit)
            scaled = jnp.where(inside, unit, 0.0) * jnp.concatenate([inverse_pivots] * (size // 128), axis=1)
            step = dot(scaled, unit, ((0,), (0,)), HIGHEST)
            below = work[start + wide :, :]
            lane_rest = lax.broadcasted_iota(jnp.int32, (rest, size), 1)
            inside_rest = jnp.logical_and(lane_rest >= start, lane_rest < start + wide)
            change = dot(jnp.where(inside_rest, below, 0.0), step, precision=HIGHEST)
            work[start + wide :, :] = jnp.where(inside_rest, 0.0, below) - change


def basis_kernel(gram, sketch, share, core_t, basis, update, work):
    size = gram.shape[0]
    work[...] = gram[...]
    turned = share[...].T
    for p in range(16):
        high, low = divmod(p, 8)
        lower = turned[high * 64 : high * 64 + 32, low : low + 1] * core_t[0:1, :]
        update[p] = lower + turned[high * 64 + 32 : high * 64 + 64, low : low + 1] * core_t[1:2, :]
    eliminate(work, size)
    row = lax.broadcasted_iota(jnp.int32, (size, size), 0)
    lane = lax.broadcasted_iota(jnp.int32, (size, size), 1)
    whole = work[...]
    pivots = jnp.sum(jnp.where(row == lane, whole, 0.0), axis=1, keepdims=True)
    inverse = jnp.where(lane < row, whole, jnp.where(lane == row, 1.0, 0.0)) * lax.rsqrt(pivots)
    basis[...] = dot(sketch[...], inverse, ((1,), (1,)), HIGHEST)


def basis_of(gram, sketch, share, core_t):
    vmem = pl.BlockSpec(memory_space=pltpu.VMEM)
    return pl.pallas_call(
        basis_kernel,
        out_shape=[jax.ShapeDtypeStruct(sketch.shape, F32), jax.ShapeDtypeStruct((16, 32, core_t.shape[1]), F32)],
        in_specs=[vmem] * 4,
        out_specs=[vmem] * 2,
        scratch_shapes=[pltpu.VMEM(gram.shape, F32)],
    )(gram, sketch, share, core_t)


def body(slab, slot_tiles, live_counts, first_prior, second_prior, first_t, second_t, third_t, core_f, core_s, core_t):
    first_sketch, second_sketch, third_sketch, gram, share = all_sums(
        slot_tiles, live_counts, slab, first_t, second_t, third_t, core_f, core_s, first_prior, second_prior
    )
    first_basis, core_update = basis_of(gram, first_sketch, share, core_t.astype(F32).T)
    return (first_sketch, second_sketch, third_sketch.reshape(2, -1), core_update, first_basis)


def solution(mesh):
    both, swapped = P(("row", "col"), None), P(("col", "row"), None)
    return jax.shard_map(
        body,
        mesh=mesh,
        in_specs=(
            P("row", "col"), P("row", "col"), P("row", "col"), both, swapped,
            P("row", None), P("col", None), P(), P(None, "row"), P("col", None), P(),
        ),
        out_specs=(both, swapped, P(), P("row", "col", None), both),
        check_vma=False,
    )
```

```python
import functools

import jax
import jax.numpy as jnp
from jax import lax
from jax.experimental import pallas as pl
from jax.experimental.pallas import tpu as pltpu
from jax.sharding import PartitionSpec as P

F32 = jnp.float32
BF16 = jnp.bfloat16
HIGHEST = lax.Precision.HIGHEST


def dot(a, b, dims=((1,), (0,)), precision=None):
    return lax.dot_general(a, b, (dims, ((), ())), precision=precision, preferred_element_type=F32)


MESH = pl.DeviceIdType.MESH
SIDE = 4
CUTS = 2
WIDE = 64
GROUP = 16


def ring_order(count):
    return sorted(range(1, count), key=lambda step: -min(step, count - step))


class Sender:
    def __init__(self, send_sems, recv_sems):
        self.send_sems, self.recv_sems, self.copies = send_sems, recv_sems, []

    def __call__(self, source, target, device):
        at = len(self.copies)
        copy = pltpu.make_async_remote_copy(
            src_ref=source, dst_ref=target, send_sem=self.send_sems.at[at], recv_sem=self.recv_sems.at[at],
            device_id=device, device_id_type=MESH,
        )
        copy.start()
        self.copies.append(copy)
        return copy


def arrive(copies):
    for copy in copies:
        copy.wait_recv()


def sums_kernel(
    tiles_h, live_h, slab_h, first_h, second_h, third_h, core_f_h, core_s_h, first_prior, second_prior,
    first_o, second_o, third_o, gram_o, share_o,
    tiles_ref, live_ref, slab, first_t, second_t, third_t, core_f, core_s, dense, region,
    first_v, second_v, core_v, third_v, down_far, down_near, up_far, up_near, second_c, core_c, third_c,
    second_1, core_1, second_2, core_2, third_xy, third_z,
    gram_v, gram_c, gram_xy, gram_own, gram_z, gram_done, pieces, pieces_in,
    load_sems, send_sems, recv_sems,
):
    tile = slab.shape[1] // 2
    slots = slab.shape[0] // tile
    rows, cols = first_t.shape[0], second_t.shape[0]
    tile_cols = cols // tile
    width = core_s.shape[1]
    factor = first_t.shape[1]
    row, z = lax.axis_index("row"), lax.axis_index("col")
    rings = lax.axis_size("col")
    core = row % 2
    chip = row // 2
    y, x = chip // SIDE, chip % SIDE
    chips = SIDE * SIDE

    loads = [
        pltpu.make_async_copy(source, target, load_sems.at[i])
        for i, (source, target) in enumerate(
            ((slab_h, slab), (third_h, third_t), (second_h, second_t), (core_s_h, core_s), (core_f_h, core_f), (first_h, first_t), (tiles_h, tiles_ref), (live_h, live_ref))
        )
    ]
    for load in loads[6:] + loads[:6]:
        load.start()

    def at_chip(dy, dx):
        return ((((y + dy) % SIDE) * SIDE + (x + dx) % SIDE) * 2 + core, z)

    def at_ring(step):
        return (row, (z + step + rings) % rings)

    partner = (chip * 2 + 1 - core, z)
    offsets = sorted(
        [(dy, dx) for dy in range(SIDE) for dx in range(SIDE) if dy or dx],
        key=lambda o: -(min(o[0], SIDE - o[0]) + min(o[1], SIDE - o[1])),
    )
    barrier = pltpu.get_barrier_semaphore()
    others = [partner] + [at_chip(*o) for o in offsets if not (o[0] and o[1])] + [at_ring(s) for s in (-2, -1, 1, 2)]
    for device in others:
        pl.semaphore_signal(barrier, inc=1, device_id=device, device_id_type=MESH)

    send = Sender(send_sems, recv_sems)
    loads[6].wait()
    loads[7].wait()
    live = live_ref[0, 0]
    places = (rows // tile) * tile_cols
    weights = [
        [jnp.logical_and(tiles_ref[s, 0] == t, s < live).astype(jnp.int32).astype(F32).astype(BF16) for s in range(slots)]
        for t in range(places)
    ]
    loads[0].wait()

    def place_rows(i, carry):
        blocks = [slab[pl.ds(pl.multiple_of(s * tile + i * 16, 16), 16), :] for s in range(slots)]
        for t in range(places):
            block = blocks[0] * weights[t][0]
            for s in range(1, slots):
                block = block + blocks[s] * weights[t][s]
            tr, tc = t // tile_cols, t % tile_cols
            at = pl.ds(pl.multiple_of(tr * tile + i * 16, 16), 16)
            dense[at, tc * tile : (tc + 1) * tile] = block[:, :tile]
            dense[at, cols + tc * tile : cols + (tc + 1) * tile] = block[:, tile:]
        return carry

    lax.fori_loop(0, tile // 16, place_rows, 0)
    loads[1].wait()
    loads[2].wait()
    third = third_t[...].astype(F32)
    halves = [dense.at[:, level * cols : (level + 1) * cols] for level in range(2)]
    first_sum = None
    for level in range(2):
        mixed = (third[level : level + 1, :] * second_t[...].astype(F32)).astype(BF16)
        term = dot(halves[level][...], mixed)
        first_sum = term if level == 0 else first_sum + term
    span = rows // rings
    first_v[...] = first_sum.reshape(rings, span, factor)
    pl.semaphore_wait(barrier, len(others))

    half = rings // 2
    cuts = [pl.ds(i * span // CUTS, span // CUTS) for i in range(CUTS)]

    def own(sign, distance):
        return (z - sign * distance + rings) % rings

    def leaf(sign, distance, hops, landing, slot):
        return [send(first_v.at[own(sign, distance), cut], landing.at[slot, cut], at_ring(-sign * hops)) for cut in cuts]

    down_runs = [leaf(1, half, 2, down_far, 0)]
    down_joins = [leaf(1, half - 1, 1, down_near, 0)]
    up_runs = [[]]
    up_joins = [leaf(-1, half - 1, 1, up_near, 0)]

    def relay(stop):
        distance = half - 2 * stop
        down_next, up_next = [], []
        for i, cut in enumerate(cuts):
            arrive([down_runs[-1][i], down_joins[-1][i]])
            down_far[stop - 1, cut] = down_far[stop - 1, cut] + down_near[stop - 1, cut] + first_v[own(1, distance), cut]
            down_next.append(send(down_far.at[stop - 1, cut], down_far.at[stop, cut], at_ring(-2)))
            up_joins[-1][i].wait_recv()
            total = up_near[stop - 1, cut] + first_v[own(-1, distance), cut]
            if stop > 1:
                up_runs[-1][i].wait_recv()
                total = total + up_far[stop - 1, cut]
            up_far[stop - 1, cut] = total
            up_next.append(send(up_far.at[stop - 1, cut], up_far.at[stop, cut], at_ring(2)))
        down_runs.append(down_next)
        up_runs.append(up_next)
        down_joins.append(leaf(1, distance - 1, 1, down_near, stop))
        up_joins.append(leaf(-1, distance - 1, 1, up_near, stop))

    loads[3].wait()
    for level in range(2):
        region[:, level * width : (level + 1) * width] = dot(halves[level][...], core_s[...]).astype(BF16)
    loads[4].wait()
    core_v[...] = dot(core_f[...], region[...]).reshape(core_v.shape)
    core_swap = send(core_v.at[:, :, 1 - core], core_c, partner)
    loads[5].wait()
    second_sum = None
    for level in range(2):
        mixed = (first_t[...].astype(F32) * third[level : level + 1, :]).astype(BF16)
        term = dot(halves[level][...], mixed, ((0,), (0,)))
        second_sum = term if level == 0 else second_sum + term
    second_v[...] = second_sum.reshape(second_v.shape)
    second_swap = send(second_v.at[:, :, 1 - core], second_c, partner)
    for level in range(2):
        across = dot(halves[level][...], second_t[...])
        third_v[0:1, level * factor : (level + 1) * factor] = jnp.sum(across * first_t[...].astype(F32), axis=0, keepdims=True)
    third_swap = send(third_v, third_c.at[core], partner)
    relay(1)

    def start_xy(total, landing):
        rows_half = total.shape[2] // 2
        copies = []
        for step in (2, 1, 3):
            to_x, to_y = (x + step) % SIDE, (y + step) % SIDE
            copies.append(send(total.at[:, to_x, 0:rows_half], landing.at[0, step - 1], at_chip(0, step)))
            copies.append(send(total.at[to_y, :, rows_half:], landing.at[1, step - 1], at_chip(step, 0)))
        return copies

    def middle_xy(total, landing, last):
        rows_half = total.shape[2] // 2
        landing[0, 0] = total[:, x, 0:rows_half] + landing[0, 0] + landing[0, 1] + landing[0, 2]
        landing[1, 0] = total[y, :, rows_half:] + landing[1, 0] + landing[1, 1] + landing[1, 2]
        copies = []
        for step in (2, 1, 3):
            to_x, to_y = (x + step) % SIDE, (y + step) % SIDE
            copies.append(send(landing.at[0, 0, to_y], last.at[0, step - 1], at_chip(step, 0)))
            copies.append(send(landing.at[1, 0, to_x], last.at[1, step - 1], at_chip(0, step)))
        return copies

    core_swap.wait_recv()
    core_c[...] = core_c[...] + core_v[:, :, core]
    core_stage = start_xy(core_c, core_1)
    relay(2)
    second_swap.wait_recv()
    second_c[...] = second_c[...] + second_v[:, :, core]
    second_stage = start_xy(second_c, second_1)
    third_swap.wait_recv()
    third_c[core] = third_v[...]
    third_xy[chip] = third_c[0] + third_c[1]
    relay(3)
    stops = half // 2
    arrive(up_runs[-1] + up_joins[-1] + down_joins[-1] + down_runs[-1])
    sketch = first_prior[...] + first_v[z] + down_near[stops - 1] + up_near[stops - 1] + up_far[stops - 1] + down_far[stops - 1]
    first_o[...] = sketch

    gram_v[...] = dot(sketch, sketch, ((0,), (0,)), HIGHEST).reshape(gram_v.shape)
    gram_swap = send(gram_v.at[1 - core], gram_c, partner)
    arrive(core_stage)
    core_last = middle_xy(core_c, core_1, core_2)
    gram_swap.wait_recv()
    gram_c[...] = gram_c[...] + gram_v[core]
    gram_stage = [
        send(gram_c.at[((y + dy) % SIDE) * SIDE + (x + dx) % SIDE], gram_xy.at[dy * SIDE + dx], at_chip(dy, dx)) for dy, dx in offsets
    ]
    arrive(second_stage)
    second_last = middle_xy(second_c, second_1, second_2)
    third_stage = [send(third_xy.at[chip], third_xy.at[chip], at_chip(*o)) for o in offsets]

    arrive(core_last)
    rows_half = core_c.shape[2] // 2
    lane = lax.broadcasted_iota(jnp.int32, (rows_half, 128), 1) // 32
    sums = [
        core_1[0, 0, y] + core_2[0, 0] + core_2[0, 1] + core_2[0, 2],
        core_1[1, 0, x] + core_2[1, 0] + core_2[1, 1] + core_2[1, 2],
    ]
    for group in range(width // 128):
        parts = [sums[k // 2][:, (k % 2) * width + group * 128 : (k % 2) * width + (group + 1) * 128] for k in range(4)]
        for m in range(4):
            piece = None
            for k in range(4):
                shift = (k - m) * 32 % 128
                moved = pltpu.roll(parts[k], shift, 1) if shift else parts[k]
                piece = moved if k == 0 else jnp.where(lane == k, moved, piece)
            pieces[group * 4 + m] = piece
    share_stage = [send(pieces.at[(z + s) % rings], pieces_in.at[s], at_ring(s)) for s in ring_order(rings)]

    arrive(gram_stage)
    total = gram_c[chip]
    for i in range(1, chips):
        total = total + gram_xy[i]
    gram_own[...] = total
    gram_ring = [send(gram_own, gram_z.at[s], at_ring(s)) for s in ring_order(rings)]
    arrive(third_stage)
    third_sum = third_xy[0]
    for i in range(1, chips):
        third_sum = third_sum + third_xy[i]
    third_z[z] = third_sum
    third_last = [send(third_z.at[z], third_z.at[z], at_ring(s)) for s in ring_order(rings)]
    arrive(second_last)
    rows_half = second_c.shape[2] // 2
    second_o[0:rows_half, :] = second_prior[0:rows_half, :] + (second_1[0, 0, y] + second_2[0, 0] + second_2[0, 1] + second_2[0, 2])
    second_o[rows_half:, :] = second_prior[rows_half:, :] + (second_1[1, 0, x] + second_2[1, 0] + second_2[1, 1] + second_2[1, 2])
    arrive(share_stage)
    share = pieces[z]
    for i in range(1, rings):
        share = share + pieces_in[i]
    share_o[...] = share
    arrive(gram_ring)
    for i in range(1, rings):
        total = total + gram_z[i]
    gram_done[core, chip] = total
    gram_spread = [send(gram_done.at[core, chip], gram_done.at[core, chip], at_chip(*o)) for o in offsets]
    arrive(third_last)
    third_sum = third_z[0]
    for i in range(1, rings):
        third_sum = third_sum + third_z[i]
    third_o[...] = third_sum
    arrive(gram_spread)
    gram_back = send(gram_done.at[core], gram_done.at[core], partner)
    gram_back.wait_recv()
    gram_o[...] = gram_done[...].reshape(gram_o.shape)
    for copy in send.copies:
        copy.wait_send()


def all_sums(slot_tiles, live_counts, slab, first_t, second_t, third_t, core_f, core_s, first_prior, second_prior):
    vmem, hbm = (pl.BlockSpec(memory_space=m) for m in (pltpu.VMEM, pl.ANY))
    rows, cols, factor, width = first_t.shape[0], second_t.shape[0], first_t.shape[1], core_s.shape[1]
    rings = lax.axis_size("col")
    chips = SIDE * SIDE
    owned, high = second_prior.shape[0], core_f.shape[0] // lax.axis_size("row")
    span = rows // rings
    half = rings // 2

    def f32(*shape):
        return pltpu.VMEM(shape, F32)

    scratch = [
        pltpu.SMEM(slot_tiles.shape, jnp.int32), pltpu.SMEM(live_counts.shape, jnp.int32),
        *(pltpu.VMEM(a.shape, BF16) for a in (slab, first_t, second_t, third_t, core_f, core_s)),
        pltpu.VMEM((rows, 2 * cols), BF16), pltpu.VMEM((rows, 2 * width), BF16),
        f32(rings, span, factor), f32(SIDE, SIDE, 2, owned, factor), f32(SIDE, SIDE, 2, high, 2 * width), f32(1, 2 * factor),
        *(f32(half // 2, span, factor) for _ in range(4)),
        f32(SIDE, SIDE, owned, factor), f32(SIDE, SIDE, high, 2 * width), f32(2, 1, 2 * factor),
        f32(2, SIDE - 1, SIDE, owned // 2, factor), f32(2, SIDE - 1, SIDE, high // 2, 2 * width),
        f32(2, SIDE - 1, owned // 2, factor), f32(2, SIDE - 1, high // 2, 2 * width),
        f32(chips, 1, 2 * factor), f32(rings, 1, 2 * factor),
        f32(2, chips, 8, factor), f32(chips, 8, factor), f32(chips, 8, factor), f32(8, factor), f32(rings, 8, factor),
        f32(2, chips, 8, factor), f32(rings, 8, 128), f32(rings, 8, 128),
        pltpu.SemaphoreType.DMA((8,)), pltpu.SemaphoreType.DMA((160,)), pltpu.SemaphoreType.DMA((160,)),
    ]
    shapes = (first_prior.shape, second_prior.shape, (1, 2 * factor), (factor, factor), (8, 128))
    return pl.pallas_call(
        sums_kernel,
        out_shape=[jax.ShapeDtypeStruct(s, F32) for s in shapes],
        in_specs=[hbm] * 8 + [vmem] * 2,
        out_specs=[vmem] * 5,
        scratch_shapes=scratch,
        compiler_params=pltpu.CompilerParams(collective_id=0, has_side_effects=True, vmem_limit_bytes=60 * 2**20),
    )(slot_tiles, live_counts, slab, first_t, second_t, third_t, core_f, core_s, first_prior, second_prior)


def eliminate(work, reciprocals, size, wide=64, group=16):
    lanes = size // 128

    def across(value):
        return jnp.concatenate([value] * lanes, axis=1)

    for start in range(0, size, wide):
        panel = work[start : start + wide, :]
        finished = []
        inverses = []
        for base in range(0, wide, group):
            high = wide - base
            at = start + base
            row_at = lax.broadcasted_iota(jnp.int32, (high, 128), 0)
            row_low = lax.broadcasted_iota(jnp.int32, (high, size), 0)
            lane_low = lax.broadcasted_iota(jnp.int32, (high, size), 1) - at
            group_row = lax.broadcasted_iota(jnp.int32, (group, 128), 0)
            inverse = jnp.zeros((group, 128), F32)
            columns = [jnp.broadcast_to(panel[:, at + k : at + k + 1], (high, 128)) for k in range(group)]
            taken = jnp.logical_and(lane_low >= 0, lane_low < group)
            panel = jnp.where(taken, jnp.where(lane_low == row_low, 1.0, 0.0), panel)
            for k in range(0, group, 2):
                one, two = columns[k], columns[k + 1]
                a, b, d = one[k : k + 1, :], two[k : k + 1, :], two[k + 1 : k + 2, :]
                inverse_one = 1.0 / a
                inverse_two = a / (a * d - b * b)
                inverse = jnp.where(group_row == k, inverse_one, jnp.where(group_row == k + 1, inverse_two, inverse))
                factor_one = jnp.where(row_at > k, one * inverse_one, 0.0)
                factor_two = jnp.where(row_at > k + 1, (two - factor_one * b) * inverse_two, 0.0)
                for later in range(k + 2, group):
                    value = columns[later] - factor_one * columns[later][k : k + 1, :]
                    columns[later] = value - factor_two * value[k + 1 : k + 2, :]
                panel = panel - across(factor_one) * panel[k : k + 1, :]
                panel = panel - across(factor_two) * panel[k + 1 : k + 2, :]
            finished.append(panel[:group])
            inverses.append(inverse)
            panel = panel[group:]
        panel = jnp.concatenate(finished, axis=0)
        inverse = jnp.concatenate(inverses, axis=0)
        reciprocals[start : start + wide, :] = inverse
        row_full = lax.broadcasted_iota(jnp.int32, (wide, size), 0)
        lane_full = lax.broadcasted_iota(jnp.int32, (wide, size), 1) - start
        panel = jnp.where(lane_full > row_full, jnp.where(lane_full < wide, 0.0, panel), panel)
        work[start : start + wide, :] = panel
        rest = size - start - wide
        if rest:
            inside = jnp.logical_and(lane_full >= 0, lane_full < wide)
            scaled = jnp.where(inside, panel, 0.0) * across(inverse)
            step = dot(scaled, panel, ((0,), (0,)), HIGHEST)
            below = work[start + wide :, :]
            lane_rest = lax.broadcasted_iota(jnp.int32, (rest, size), 1) - start
            inside_rest = jnp.logical_and(lane_rest >= 0, lane_rest < wide)
            change = dot(jnp.where(inside_rest, below, 0.0), step, precision=HIGHEST)
            work[start + wide :, :] = jnp.where(inside_rest, 0.0, below) - change


def inverse_factor(gram, work, reciprocals):
    size = gram.shape[0]
    row = lax.broadcasted_iota(jnp.int32, (size, size), 0)
    lane = lax.broadcasted_iota(jnp.int32, (size, size), 1)
    whole = gram[...]
    diagonal = jnp.where(row == lane, whole, 0.0)
    along = lax.rsqrt(jnp.sum(diagonal, axis=0, keepdims=True))
    work[...] = jnp.where(row == lane, 1.0, whole * along * lax.rsqrt(jnp.sum(diagonal, axis=1, keepdims=True)))
    eliminate(work, reciprocals, size, WIDE, GROUP)
    scale = jnp.concatenate([jnp.sqrt(reciprocals[...])] * (size // 128), axis=1)
    return jnp.where(lane <= row, work[...], 0.0) * scale * along


def basis_kernel(
    gram, sketch, second, third, share, core_t, sketch_o, second_o, third_o, update_o, basis, work, reciprocals, update, sem
):
    turned = share[...].T
    core_rows = core_t[...].astype(F32).T
    for p in range(16):
        high, low = divmod(p, 8)
        lower = turned[high * 64 : high * 64 + 32, low : low + 1] * core_rows[0:1, :]
        update[p] = lower + turned[high * 64 + 32 : high * 64 + 64, low : low + 1] * core_rows[1:2, :]
    store = pltpu.make_async_copy(update, update_o, sem)
    store.start()
    factor = third_o.shape[1]
    sketch_o[...] = sketch[...]
    second_o[...] = second[...]
    third_o[0:1, :] = third[:, :factor]
    third_o[1:2, :] = third[:, factor:]
    basis[...] = dot(sketch[...], inverse_factor(gram, work, reciprocals), ((1,), (1,)), HIGHEST)
    store.wait()


def basis_of(gram, sketch, second, third, share, core_t):
    vmem, hbm = pl.BlockSpec(memory_space=pltpu.VMEM), pl.BlockSpec(memory_space=pl.ANY)
    update = (16, 32, core_t.shape[0])
    shapes = (sketch.shape, second.shape, (2, third.shape[1] // 2), update, sketch.shape)
    return pl.pallas_call(
        basis_kernel,
        out_shape=[jax.ShapeDtypeStruct(s, F32) for s in shapes],
        in_specs=[vmem] * 6,
        out_specs=[vmem, vmem, vmem, hbm, vmem],
        scratch_shapes=[
            pltpu.VMEM(gram.shape, F32), pltpu.VMEM((gram.shape[0], 128), F32), pltpu.VMEM(update, F32), pltpu.SemaphoreType.DMA,
        ],
    )(gram, sketch, second, third, share, core_t)


def body(slab, slot_tiles, live_counts, first_prior, second_prior, first_t, second_t, third_t, core_f, core_s, core_t):
    first_sums, second_sums, third_sums, gram, share = all_sums(
        slot_tiles, live_counts, slab, first_t, second_t, third_t, core_f, core_s, first_prior, second_prior
    )
    first_sketch, second_sketch, third_sketch, core_update, first_basis = basis_of(
        gram, first_sums, second_sums, third_sums, share, core_t
    )
    return (first_sketch, second_sketch, third_sketch, core_update, first_basis)


def solution(mesh):
    both, swapped = P(("row", "col"), None), P(("col", "row"), None)
    return jax.shard_map(
        body,
        mesh=mesh,
        in_specs=(
            P("row", "col"), P("row", "col"), P("row", "col"), both, swapped,
            P("row", None), P("col", None), P(), P(None, "row"), P("col", None), P(),
        ),
        out_specs=(both, swapped, P(), P("row", "col", None), both),
        check_vma=False,
    )
```

```python
import functools

import jax
import jax.numpy as jnp
from jax import lax
from jax.experimental import pallas as pl
from jax.experimental.pallas import tpu as pltpu
from jax.sharding import PartitionSpec as P

F32 = jnp.float32
BF16 = jnp.bfloat16
HIGHEST = lax.Precision.HIGHEST


def dot(a, b, dims=((1,), (0,)), precision=None):
    return lax.dot_general(a, b, (dims, ((), ())), precision=precision, preferred_element_type=F32)


MESH = pl.DeviceIdType.MESH
SIDE = 4
CUTS = 2
WIDE = 64
GROUP = 16


def ring_order(count):
    return sorted(range(1, count), key=lambda step: -min(step, count - step))


class Sender:
    def __init__(self, send_sems, recv_sems):
        self.send_sems, self.recv_sems, self.copies = send_sems, recv_sems, []

    def __call__(self, source, target, device):
        at = len(self.copies)
        copy = pltpu.make_async_remote_copy(
            src_ref=source, dst_ref=target, send_sem=self.send_sems.at[at], recv_sem=self.recv_sems.at[at],
            device_id=device, device_id_type=MESH,
        )
        copy.start()
        self.copies.append(copy)
        return copy


def arrive(copies):
    for copy in copies:
        copy.wait_recv()


def sums_kernel(
    tiles_h, live_h, slab_h, first_h, second_h, third_h, core_f_h, core_s_h, first_prior, second_prior,
    first_o, second_o, third_o, gram_o, share_o,
    tiles_ref, live_ref, slab, first_t, second_t, third_t, core_f, core_s, mixed, dense, region,
    first_v, second_v, core_v, third_v, down_far, down_near, up_far, up_near, second_c, core_c, third_c,
    second_1, core_1, second_2, core_2, third_xy, third_z,
    gram_v, gram_c, gram_xy, gram_own, gram_z, gram_done, pieces, pieces_in,
    load_sems, send_sems, recv_sems,
):
    tile = slab.shape[1] // 2
    slots = slab.shape[0] // tile
    rows, cols = first_t.shape[0], second_t.shape[0]
    tile_cols = cols // tile
    width = core_s.shape[1]
    factor = first_t.shape[1]
    row, z = lax.axis_index("row"), lax.axis_index("col")
    rings = lax.axis_size("col")
    core = row % 2
    chip = row // 2
    y, x = chip // SIDE, chip % SIDE
    chips = SIDE * SIDE

    def load(source, target, at):
        return pltpu.make_async_copy(source, target, load_sems.at[at])

    early = [load(third_h, third_t, 0), load(second_h, second_t, 1), load(tiles_h, tiles_ref, 2), load(live_h, live_ref, 3)]
    blocks_in = [load(slab_h.at[s * tile : (s + 1) * tile], slab.at[s * tile : (s + 1) * tile], 4 + s) for s in range(slots)]
    late = [load(core_s_h, core_s, 4 + slots), load(core_f_h, core_f, 5 + slots), load(first_h, first_t, 6 + slots)]
    for copy in early + blocks_in + late:
        copy.start()

    def at_chip(dy, dx):
        return ((((y + dy) % SIDE) * SIDE + (x + dx) % SIDE) * 2 + core, z)

    def at_ring(step):
        return (row, (z + step + rings) % rings)

    partner = (chip * 2 + 1 - core, z)
    offsets = sorted(
        [(dy, dx) for dy in range(SIDE) for dx in range(SIDE) if dy or dx],
        key=lambda o: -(min(o[0], SIDE - o[0]) + min(o[1], SIDE - o[1])),
    )
    barrier = pltpu.get_barrier_semaphore()
    others = [partner] + [at_chip(*o) for o in offsets] + [at_ring(s) for s in (-2, -1, 1, 2)]
    for device in others:
        pl.semaphore_signal(barrier, inc=1, device_id=device, device_id_type=MESH)

    send = Sender(send_sems, recv_sems)
    early[0].wait()
    early[1].wait()
    third = third_t[...].astype(F32)
    for level in range(2):
        mixed[level] = (third[level : level + 1, :] * second_t[...].astype(F32)).astype(BF16)
    early[2].wait()
    early[3].wait()
    live = live_ref[0, 0]
    places = (rows // tile) * tile_cols
    weights = [
        [jnp.logical_and(tiles_ref[0, s] == t, s < live).astype(jnp.int32).astype(F32).astype(BF16) for s in range(slots)]
        for t in range(places)
    ]
    for copy in blocks_in:
        copy.wait()
    for t in range(places):
        block = slab[0:tile, :] * weights[t][0]
        for s in range(1, slots):
            block = block + slab[s * tile : (s + 1) * tile, :] * weights[t][s]
        at, tc = pl.ds(t // tile_cols * tile, tile), t % tile_cols
        dense[at, tc * tile : (tc + 1) * tile] = block[:, :tile]
        dense[at, cols + tc * tile : cols + (tc + 1) * tile] = block[:, tile:]
    halves = [dense.at[:, level * cols : (level + 1) * cols] for level in range(2)]
    first_sum = dot(halves[0][...], mixed[0]) + dot(halves[1][...], mixed[1])
    span = rows // rings
    first_v[...] = first_sum.reshape(rings, span, factor)
    pl.semaphore_wait(barrier, len(others))

    half = rings // 2
    cuts = [pl.ds(i * span // CUTS, span // CUTS) for i in range(CUTS)]

    def own(sign, distance):
        return (z - sign * distance + rings) % rings

    def leaf(sign, distance, hops, landing, slot):
        return [send(first_v.at[own(sign, distance), cut], landing.at[slot, cut], at_ring(-sign * hops)) for cut in cuts]

    down_runs = [leaf(1, half, 2, down_far, 0)]
    down_joins = [leaf(1, half - 1, 1, down_near, 0)]
    up_runs = [[]]
    up_joins = [leaf(-1, half - 1, 1, up_near, 0)]

    def relay(stop):
        distance = half - 2 * stop
        down_next, up_next = [], []
        for i, cut in enumerate(cuts):
            arrive([down_runs[-1][i], down_joins[-1][i]])
            down_far[stop - 1, cut] = down_far[stop - 1, cut] + down_near[stop - 1, cut] + first_v[own(1, distance), cut]
            down_next.append(send(down_far.at[stop - 1, cut], down_far.at[stop, cut], at_ring(-2)))
            up_joins[-1][i].wait_recv()
            total = up_near[stop - 1, cut] + first_v[own(-1, distance), cut]
            if stop > 1:
                up_runs[-1][i].wait_recv()
                total = total + up_far[stop - 1, cut]
            up_far[stop - 1, cut] = total
            up_next.append(send(up_far.at[stop - 1, cut], up_far.at[stop, cut], at_ring(2)))
        down_runs.append(down_next)
        up_runs.append(up_next)
        down_joins.append(leaf(1, distance - 1, 1, down_near, stop))
        up_joins.append(leaf(-1, distance - 1, 1, up_near, stop))

    late[0].wait()
    for level in range(2):
        region[:, level * width : (level + 1) * width] = dot(halves[level][...], core_s[...]).astype(BF16)
    late[1].wait()
    core_v[...] = dot(core_f[...], region[...]).reshape(core_v.shape)
    core_swap = send(core_v.at[:, :, 1 - core], core_c, partner)
    late[2].wait()
    second_sum = None
    for level in range(2):
        weights = (first_t[...].astype(F32) * third[level : level + 1, :]).astype(BF16)
        term = dot(halves[level][...], weights, ((0,), (0,)))
        second_sum = term if level == 0 else second_sum + term
    second_v[...] = second_sum.reshape(second_v.shape)
    second_swap = send(second_v.at[:, :, 1 - core], second_c, partner)
    for level in range(2):
        across = dot(halves[level][...], second_t[...])
        third_v[0:1, level * factor : (level + 1) * factor] = jnp.sum(across * first_t[...].astype(F32), axis=0, keepdims=True)
    third_swap = send(third_v, third_c.at[core], partner)
    relay(1)

    def start_xy(total, landing):
        rows_half = total.shape[2] // 2
        copies = []
        for step in (2, 1, 3):
            to_x, to_y = (x + step) % SIDE, (y + step) % SIDE
            copies.append(send(total.at[:, to_x, 0:rows_half], landing.at[0, step - 1], at_chip(0, step)))
            copies.append(send(total.at[to_y, :, rows_half:], landing.at[1, step - 1], at_chip(step, 0)))
        return copies

    def middle_xy(total, landing, last):
        rows_half = total.shape[2] // 2
        landing[0, 0] = total[:, x, 0:rows_half] + landing[0, 0] + landing[0, 1] + landing[0, 2]
        landing[1, 0] = total[y, :, rows_half:] + landing[1, 0] + landing[1, 1] + landing[1, 2]
        copies = []
        for step in (2, 1, 3):
            to_x, to_y = (x + step) % SIDE, (y + step) % SIDE
            copies.append(send(landing.at[0, 0, to_y], last.at[0, step - 1], at_chip(step, 0)))
            copies.append(send(landing.at[1, 0, to_x], last.at[1, step - 1], at_chip(0, step)))
        return copies

    core_swap.wait_recv()
    core_c[...] = core_c[...] + core_v[:, :, core]
    core_stage = start_xy(core_c, core_1)
    relay(2)
    second_swap.wait_recv()
    second_c[...] = second_c[...] + second_v[:, :, core]
    second_stage = start_xy(second_c, second_1)
    third_swap.wait_recv()
    third_c[core] = third_v[...]
    third_xy[chip] = third_c[0] + third_c[1]
    relay(3)
    stops = half // 2
    arrive(up_runs[-1] + up_joins[-1] + down_joins[-1] + down_runs[-1])
    sketch = first_prior[...] + first_v[z] + down_near[stops - 1] + up_near[stops - 1] + up_far[stops - 1] + down_far[stops - 1]
    first_o[...] = sketch

    gram_v[...] = dot(sketch, sketch, ((0,), (0,)), HIGHEST).reshape(gram_v.shape)
    gram_swap = send(gram_v.at[1 - core], gram_c, partner)
    gram_swap.wait_recv()
    gram_c[...] = gram_c[...] + gram_v[core]
    gram_stage = [
        send(gram_c.at[((y + dy) % SIDE) * SIDE + (x + dx) % SIDE], gram_xy.at[dy * SIDE + dx], at_chip(dy, dx)) for dy, dx in offsets
    ]
    arrive(core_stage)
    core_last = middle_xy(core_c, core_1, core_2)
    arrive(second_stage)
    second_last = middle_xy(second_c, second_1, second_2)
    third_stage = [send(third_xy.at[chip], third_xy.at[chip], at_chip(*o)) for o in offsets]

    arrive(gram_stage)
    total = gram_c[chip]
    for i in range(1, chips):
        total = total + gram_xy[i]
    gram_own[...] = total
    gram_ring = [send(gram_own, gram_z.at[s], at_ring(s)) for s in ring_order(rings)]
    arrive(third_stage)
    third_sum = third_xy[0]
    for i in range(1, chips):
        third_sum = third_sum + third_xy[i]
    third_z[z] = third_sum
    third_last = [send(third_z.at[z], third_z.at[z], at_ring(s)) for s in ring_order(rings)]

    arrive(core_last)
    rows_half = core_c.shape[2] // 2
    lane = lax.broadcasted_iota(jnp.int32, (rows_half, 128), 1) // 32
    sums = [
        core_1[0, 0, y] + core_2[0, 0] + core_2[0, 1] + core_2[0, 2],
        core_1[1, 0, x] + core_2[1, 0] + core_2[1, 1] + core_2[1, 2],
    ]
    for group in range(width // 128):
        parts = [sums[k // 2][:, (k % 2) * width + group * 128 : (k % 2) * width + (group + 1) * 128] for k in range(4)]
        for m in range(4):
            piece = None
            for k in range(4):
                shift = (k - m) * 32 % 128
                moved = pltpu.roll(parts[k], shift, 1) if shift else parts[k]
                piece = moved if k == 0 else jnp.where(lane == k, moved, piece)
            pieces[group * 4 + m] = piece
    share_stage = [send(pieces.at[(z + s) % rings], pieces_in.at[s], at_ring(s)) for s in ring_order(rings)]
    arrive(second_last)
    rows_half = second_c.shape[2] // 2
    second_o[0:rows_half, :] = second_prior[0:rows_half, :] + (second_1[0, 0, y] + second_2[0, 0] + second_2[0, 1] + second_2[0, 2])
    second_o[rows_half:, :] = second_prior[rows_half:, :] + (second_1[1, 0, x] + second_2[1, 0] + second_2[1, 1] + second_2[1, 2])

    arrive(gram_ring)
    for i in range(1, rings):
        total = total + gram_z[i]
    gram_done[core, chip] = total
    gram_spread = [send(gram_done.at[core, chip], gram_done.at[core, chip], at_chip(*o)) for o in offsets]
    arrive(gram_spread)
    gram_back = send(gram_done.at[core], gram_done.at[core], partner)
    arrive(share_stage)
    share = pieces[z]
    for i in range(1, rings):
        share = share + pieces_in[i]
    share_o[...] = share
    arrive(third_last)
    third_sum = third_z[0]
    for i in range(1, rings):
        third_sum = third_sum + third_z[i]
    third_o[...] = third_sum
    gram_back.wait_recv()
    gram_o[...] = gram_done[...].reshape(gram_o.shape)
    for copy in send.copies:
        copy.wait_send()


def all_sums(slot_tiles, live_counts, slab, first_t, second_t, third_t, core_f, core_s, first_prior, second_prior):
    vmem, hbm = (pl.BlockSpec(memory_space=m) for m in (pltpu.VMEM, pl.ANY))
    rows, cols, factor, width = first_t.shape[0], second_t.shape[0], first_t.shape[1], core_s.shape[1]
    rings = lax.axis_size("col")
    chips = SIDE * SIDE
    owned, high = second_prior.shape[0], core_f.shape[0] // lax.axis_size("row")
    span = rows // rings
    half = rings // 2

    def f32(*shape):
        return pltpu.VMEM(shape, F32)

    scratch = [
        pltpu.SMEM(slot_tiles.shape, jnp.int32), pltpu.SMEM(live_counts.shape, jnp.int32),
        *(pltpu.VMEM(a.shape, BF16) for a in (slab, first_t, second_t, third_t, core_f, core_s)),
        pltpu.VMEM((2, *second_t.shape), BF16), pltpu.VMEM((rows, 2 * cols), BF16), pltpu.VMEM((rows, 2 * width), BF16),
        f32(rings, span, factor), f32(SIDE, SIDE, 2, owned, factor), f32(SIDE, SIDE, 2, high, 2 * width), f32(1, 2 * factor),
        *(f32(half // 2, span, factor) for _ in range(4)),
        f32(SIDE, SIDE, owned, factor), f32(SIDE, SIDE, high, 2 * width), f32(2, 1, 2 * factor),
        f32(2, SIDE - 1, SIDE, owned // 2, factor), f32(2, SIDE - 1, SIDE, high // 2, 2 * width),
        f32(2, SIDE - 1, owned // 2, factor), f32(2, SIDE - 1, high // 2, 2 * width),
        f32(chips, 1, 2 * factor), f32(rings, 1, 2 * factor),
        f32(2, chips, 8, factor), f32(chips, 8, factor), f32(chips, 8, factor), f32(8, factor), f32(rings, 8, factor),
        f32(2, chips, 8, factor), f32(rings, 8, 128), f32(rings, 8, 128),
        pltpu.SemaphoreType.DMA((16,)), pltpu.SemaphoreType.DMA((160,)), pltpu.SemaphoreType.DMA((160,)),
    ]
    shapes = (first_prior.shape, second_prior.shape, (1, 2 * factor), (factor, factor), (8, 128))
    return pl.pallas_call(
        sums_kernel,
        out_shape=[jax.ShapeDtypeStruct(s, F32) for s in shapes],
        in_specs=[hbm] * 8 + [vmem] * 2,
        out_specs=[vmem] * 5,
        scratch_shapes=scratch,
        compiler_params=pltpu.CompilerParams(collective_id=0, has_side_effects=True, vmem_limit_bytes=60 * 2**20),
    )(slot_tiles, live_counts, slab, first_t, second_t, third_t, core_f, core_s, first_prior, second_prior)


def block_lanes(rows, start, wide):
    shift = start % 128
    value = rows[:, start - shift : start - shift + 128]
    return (pltpu.roll(value, 128 - shift, 1) if shift else value)[:, :wide]


def eliminate(work, reciprocals, size, wide=64, group=16):
    lanes = size // 128

    def across(value):
        return jnp.concatenate([value] * lanes, axis=1)

    for start in range(0, size, wide):
        panel = work[start : start + wide, :]
        finished = []
        inverses = []
        for base in range(0, wide, group):
            high = wide - base
            at = start + base
            row_at = lax.broadcasted_iota(jnp.int32, (high, 128), 0)
            row_low = lax.broadcasted_iota(jnp.int32, (high, size), 0)
            lane_low = lax.broadcasted_iota(jnp.int32, (high, size), 1) - at
            group_row = lax.broadcasted_iota(jnp.int32, (group, 128), 0)
            inverse = jnp.zeros((group, 128), F32)
            columns = [jnp.broadcast_to(panel[:, at + k : at + k + 1], (high, 128)) for k in range(group)]
            taken = jnp.logical_and(lane_low >= 0, lane_low < group)
            panel = jnp.where(taken, jnp.where(lane_low == row_low, 1.0, 0.0), panel)
            for k in range(0, group, 2):
                one, two = columns[k], columns[k + 1]
                a, b, d = one[k : k + 1, :], two[k : k + 1, :], two[k + 1 : k + 2, :]
                inverse_one = 1.0 / a
                inverse_two = a * (1.0 / (a * d - b * b))
                inverse = jnp.where(group_row == k, inverse_one, jnp.where(group_row == k + 1, inverse_two, inverse))
                factor_one = jnp.where(row_at > k, one * inverse_one, 0.0)
                factor_two = jnp.where(row_at > k + 1, (two - factor_one * b) * inverse_two, 0.0)
                for later in range(k + 2, group):
                    value = columns[later] - factor_one * columns[later][k : k + 1, :]
                    columns[later] = value - factor_two * value[k + 1 : k + 2, :]
                panel = panel - across(factor_one) * panel[k : k + 1, :]
                panel = panel - across(factor_two) * panel[k + 1 : k + 2, :]
            finished.append(panel[:group])
            inverses.append(inverse)
            panel = panel[group:]
        panel = jnp.concatenate(finished, axis=0)
        inverse = jnp.concatenate(inverses, axis=0)
        reciprocals[start : start + wide, :] = inverse
        row_full = lax.broadcasted_iota(jnp.int32, (wide, size), 0)
        lane_full = lax.broadcasted_iota(jnp.int32, (wide, size), 1) - start
        panel = jnp.where(lane_full > row_full, jnp.where(lane_full < wide, 0.0, panel), panel)
        work[start : start + wide, :] = panel
        rest = size - start - wide
        if rest:
            inside = jnp.logical_and(lane_full >= 0, lane_full < wide)
            scaled = block_lanes(panel, start, wide) * inverse[:, :wide]
            step = dot(scaled, panel, ((0,), (0,)), HIGHEST)
            for low in range(start + wide, size, wide):
                below = work[low : low + wide, :]
                change = dot(block_lanes(below, start, wide), step, precision=HIGHEST)
                work[low : low + wide, :] = jnp.where(inside, 0.0, below) - change


def inverse_factor(gram, work, reciprocals):
    size = gram.shape[0]
    row = lax.broadcasted_iota(jnp.int32, (size, size), 0)
    lane = lax.broadcasted_iota(jnp.int32, (size, size), 1)
    whole = gram[...]
    diagonal = jnp.where(row == lane, whole, 0.0)
    along = lax.rsqrt(jnp.sum(diagonal, axis=0, keepdims=True))
    work[...] = jnp.where(row == lane, 1.0, whole * along * lax.rsqrt(jnp.sum(diagonal, axis=1, keepdims=True)))
    eliminate(work, reciprocals, size, WIDE, GROUP)
    scale = jnp.concatenate([jnp.sqrt(reciprocals[...])] * (size // 128), axis=1)
    return jnp.where(lane <= row, work[...], 0.0) * scale * along


def basis_kernel(
    gram, sketch, second, third, share, core_t, sketch_o, second_o, third_o, update_o, basis, work, reciprocals, update, sem
):
    turned = share[...].T
    core_rows = core_t[...].astype(F32)
    for p in range(16):
        high, low = divmod(p, 8)
        lower = turned[high * 64 : high * 64 + 32, low : low + 1] * core_rows[0:1, :]
        update[p] = lower + turned[high * 64 + 32 : high * 64 + 64, low : low + 1] * core_rows[1:2, :]
    store = pltpu.make_async_copy(update, update_o, sem)
    store.start()
    factor = third_o.shape[1]
    sketch_o[...] = sketch[...]
    second_o[...] = second[...]
    third_o[0:1, :] = third[:, :factor]
    third_o[1:2, :] = third[:, factor:]
    basis[...] = dot(sketch[...], inverse_factor(gram, work, reciprocals), ((1,), (1,)), HIGHEST)
    store.wait()


def basis_of(gram, sketch, second, third, share, core_t):
    vmem, hbm = pl.BlockSpec(memory_space=pltpu.VMEM), pl.BlockSpec(memory_space=pl.ANY)
    update = (16, 32, core_t.shape[1])
    shapes = (sketch.shape, second.shape, (2, third.shape[1] // 2), update, sketch.shape)
    return pl.pallas_call(
        basis_kernel,
        out_shape=[jax.ShapeDtypeStruct(s, F32) for s in shapes],
        in_specs=[vmem] * 6,
        out_specs=[vmem, vmem, vmem, hbm, vmem],
        scratch_shapes=[
            pltpu.VMEM(gram.shape, F32), pltpu.VMEM((gram.shape[0], 128), F32), pltpu.VMEM(update, F32), pltpu.SemaphoreType.DMA,
        ],
    )(gram, sketch, second, third, share, core_t)


def body(slab, slot_tiles, live_counts, first_prior, second_prior, first_t, second_t, third_t, core_f, core_s, core_t):
    first_sums, second_sums, third_sums, gram, share = all_sums(
        slot_tiles.T, live_counts, slab, first_t, second_t, third_t, core_f, core_s, first_prior, second_prior
    )
    first_sketch, second_sketch, third_sketch, core_update, first_basis = basis_of(
        gram, first_sums, second_sums, third_sums, share, core_t.T
    )
    return (first_sketch, second_sketch, third_sketch, core_update, first_basis)


def solution(mesh):
    both, swapped = P(("row", "col"), None), P(("col", "row"), None)
    return jax.shard_map(
        body,
        mesh=mesh,
        in_specs=(
            P("row", "col"), P("row", "col"), P("row", "col"), both, swapped,
            P("row", None), P("col", None), P(), P(None, "row"), P("col", None), P(),
        ),
        out_specs=(both, swapped, P(), P("row", "col", None), both),
        check_vma=False,
    )
```

```python
import functools

import jax
import jax.numpy as jnp
from jax import lax
from jax.experimental import pallas as pl
from jax.experimental.pallas import tpu as pltpu
from jax.sharding import PartitionSpec as P

F32 = jnp.float32
BF16 = jnp.bfloat16
HIGHEST = lax.Precision.HIGHEST


def dot(a, b, dims=((1,), (0,)), precision=None):
    return lax.dot_general(a, b, (dims, ((), ())), precision=precision, preferred_element_type=F32)


MESH = pl.DeviceIdType.MESH
SIDE = 4
CUTS = 2
WIDE = 64
GROUP = 16


def ring_order(count):
    return sorted(range(1, count), key=lambda step: -min(step, count - step))


class Sender:
    def __init__(self, send_sems, recv_sems):
        self.send_sems, self.recv_sems, self.copies = send_sems, recv_sems, []

    def __call__(self, source, target, device):
        at = len(self.copies)
        copy = pltpu.make_async_remote_copy(
            src_ref=source, dst_ref=target, send_sem=self.send_sems.at[at], recv_sem=self.recv_sems.at[at],
            device_id=device, device_id_type=MESH,
        )
        copy.start()
        self.copies.append(copy)
        return copy


def arrive(copies):
    for copy in copies:
        copy.wait_recv()


def sums_kernel(
    tiles_h, live_h, slab_h, first_h, second_h, third_h, core_f_h, core_s_h, first_prior, second_prior,
    first_o, second_o, third_o, gram_o, share_o,
    tiles_ref, live_ref, slab, first_t, second_t, third_t, core_f, core_s, mixed, dense, region,
    first_v, second_v, core_v, third_v, down_far, down_near, up_far, up_near, second_c, core_c, third_c,
    second_1, core_1, second_2, core_2, third_xy, third_z,
    gram_v, gram_c, gram_xy, gram_own, gram_z, gram_done, pieces, pieces_in,
    load_sems, send_sems, recv_sems,
):
    tile = slab.shape[1] // 2
    slots = slab.shape[0] // tile
    rows, cols = first_t.shape[0], second_t.shape[0]
    tile_cols = cols // tile
    width = core_s.shape[1]
    factor = first_t.shape[1]
    row, z = lax.axis_index("row"), lax.axis_index("col")
    rings = lax.axis_size("col")
    core = row % 2
    chip = row // 2
    y, x = chip // SIDE, chip % SIDE
    chips = SIDE * SIDE

    def load(source, target, at):
        return pltpu.make_async_copy(source, target, load_sems.at[at])

    early = [load(third_h, third_t, 0), load(second_h, second_t, 1), load(tiles_h, tiles_ref, 2), load(live_h, live_ref, 3)]
    blocks_in = [load(slab_h.at[s * tile : (s + 1) * tile], slab.at[s * tile : (s + 1) * tile], 4 + s) for s in range(slots)]
    late = [load(core_s_h, core_s, 4 + slots), load(core_f_h, core_f, 5 + slots), load(first_h, first_t, 6 + slots)]
    for copy in early + blocks_in + late:
        copy.start()

    def at_chip(dy, dx):
        return ((((y + dy) % SIDE) * SIDE + (x + dx) % SIDE) * 2 + core, z)

    def at_ring(step):
        return (row, (z + step + rings) % rings)

    partner = (chip * 2 + 1 - core, z)
    offsets = sorted(
        [(dy, dx) for dy in range(SIDE) for dx in range(SIDE) if dy or dx],
        key=lambda o: -(min(o[0], SIDE - o[0]) + min(o[1], SIDE - o[1])),
    )
    barrier = pltpu.get_barrier_semaphore()
    others = [partner] + [at_chip(*o) for o in offsets] + [at_ring(s) for s in (-2, -1, 1, 2)]
    for device in others:
        pl.semaphore_signal(barrier, inc=1, device_id=device, device_id_type=MESH)

    send = Sender(send_sems, recv_sems)
    early[0].wait()
    early[1].wait()
    third = third_t[...].astype(F32)
    for level in range(2):
        mixed[level] = (third[level : level + 1, :] * second_t[...].astype(F32)).astype(BF16)
    early[2].wait()
    early[3].wait()
    live = live_ref[0, 0]
    places = (rows // tile) * tile_cols
    weights = [
        [jnp.logical_and(tiles_ref[0, s] == t, s < live).astype(jnp.int32).astype(F32).astype(BF16) for s in range(slots)]
        for t in range(places)
    ]
    for copy in blocks_in:
        copy.wait()
    for t in range(places):
        block = slab[0:tile, :] * weights[t][0]
        for s in range(1, slots):
            block = block + slab[s * tile : (s + 1) * tile, :] * weights[t][s]
        at, tc = pl.ds(t // tile_cols * tile, tile), t % tile_cols
        dense[at, tc * tile : (tc + 1) * tile] = block[:, :tile]
        dense[at, cols + tc * tile : cols + (tc + 1) * tile] = block[:, tile:]
    halves = [dense.at[:, level * cols : (level + 1) * cols] for level in range(2)]
    first_sum = dot(halves[0][...], mixed[0]) + dot(halves[1][...], mixed[1])
    span = rows // rings
    first_v[...] = first_sum.reshape(rings, span, factor)
    pl.semaphore_wait(barrier, len(others))

    half = rings // 2
    cuts = [pl.ds(i * span // CUTS, span // CUTS) for i in range(CUTS)]

    def own(sign, distance):
        return (z - sign * distance + rings) % rings

    def leaf(sign, distance, hops, landing, slot):
        return [send(first_v.at[own(sign, distance), cut], landing.at[slot, cut], at_ring(-sign * hops)) for cut in cuts]

    down_runs = [leaf(1, half, 2, down_far, 0)]
    down_joins = [leaf(1, half - 1, 1, down_near, 0)]
    up_runs = [[]]
    up_joins = [leaf(-1, half - 1, 1, up_near, 0)]

    def relay(stop):
        distance = half - 2 * stop
        down_next, up_next = [], []
        for i, cut in enumerate(cuts):
            arrive([down_runs[-1][i], down_joins[-1][i]])
            down_far[stop - 1, cut] = down_far[stop - 1, cut] + down_near[stop - 1, cut] + first_v[own(1, distance), cut]
            down_next.append(send(down_far.at[stop - 1, cut], down_far.at[stop, cut], at_ring(-2)))
            up_joins[-1][i].wait_recv()
            total = up_near[stop - 1, cut] + first_v[own(-1, distance), cut]
            if stop > 1:
                up_runs[-1][i].wait_recv()
                total = total + up_far[stop - 1, cut]
            up_far[stop - 1, cut] = total
            up_next.append(send(up_far.at[stop - 1, cut], up_far.at[stop, cut], at_ring(2)))
        down_runs.append(down_next)
        up_runs.append(up_next)
        down_joins.append(leaf(1, distance - 1, 1, down_near, stop))
        up_joins.append(leaf(-1, distance - 1, 1, up_near, stop))

    late[0].wait()
    for level in range(2):
        region[:, level * width : (level + 1) * width] = dot(halves[level][...], core_s[...]).astype(BF16)
    late[1].wait()
    core_v[...] = dot(core_f[...], region[...]).reshape(core_v.shape)
    core_swap = send(core_v.at[:, :, 1 - core], core_c, partner)
    late[2].wait()
    second_sum = None
    for level in range(2):
        weights = (first_t[...].astype(F32) * third[level : level + 1, :]).astype(BF16)
        term = dot(halves[level][...], weights, ((0,), (0,)))
        second_sum = term if level == 0 else second_sum + term
    second_v[...] = second_sum.reshape(second_v.shape)
    second_swap = send(second_v.at[:, :, 1 - core], second_c, partner)
    for level in range(2):
        across = dot(halves[level][...], second_t[...])
        third_v[0:1, level * factor : (level + 1) * factor] = jnp.sum(across * first_t[...].astype(F32), axis=0, keepdims=True)
    third_swap = send(third_v, third_c.at[core], partner)
    relay(1)

    def start_xy(total, landing):
        rows_half = total.shape[2] // 2
        copies = []
        for step in (2, 1, 3):
            to_x, to_y = (x + step) % SIDE, (y + step) % SIDE
            copies.append(send(total.at[:, to_x, 0:rows_half], landing.at[0, step - 1], at_chip(0, step)))
            copies.append(send(total.at[to_y, :, rows_half:], landing.at[1, step - 1], at_chip(step, 0)))
        return copies

    def middle_xy(total, landing, last):
        rows_half = total.shape[2] // 2
        landing[0, 0] = total[:, x, 0:rows_half] + landing[0, 0] + landing[0, 1] + landing[0, 2]
        landing[1, 0] = total[y, :, rows_half:] + landing[1, 0] + landing[1, 1] + landing[1, 2]
        copies = []
        for step in (2, 1, 3):
            to_x, to_y = (x + step) % SIDE, (y + step) % SIDE
            copies.append(send(landing.at[0, 0, to_y], last.at[0, step - 1], at_chip(step, 0)))
            copies.append(send(landing.at[1, 0, to_x], last.at[1, step - 1], at_chip(0, step)))
        return copies

    core_swap.wait_recv()
    core_c[...] = core_c[...] + core_v[:, :, core]
    core_stage = start_xy(core_c, core_1)
    relay(2)
    second_swap.wait_recv()
    second_c[...] = second_c[...] + second_v[:, :, core]
    second_stage = start_xy(second_c, second_1)
    third_swap.wait_recv()
    third_c[core] = third_v[...]
    third_xy[chip] = third_c[0] + third_c[1]
    third_stage = [send(third_xy.at[chip], third_xy.at[chip], at_chip(*o)) for o in offsets]
    relay(3)
    stops = half // 2
    arrive(up_runs[-1] + up_joins[-1] + down_joins[-1] + down_runs[-1])
    sketch = first_prior[...] + first_v[z] + down_near[stops - 1] + up_near[stops - 1] + up_far[stops - 1] + down_far[stops - 1]
    first_o[...] = sketch

    gram_v[...] = dot(sketch, sketch, ((0,), (0,)), HIGHEST).reshape(gram_v.shape)
    gram_swap = send(gram_v.at[1 - core], gram_c, partner)
    gram_swap.wait_recv()
    gram_c[...] = gram_c[...] + gram_v[core]
    gram_stage = [
        send(gram_c.at[((y + dy) % SIDE) * SIDE + (x + dx) % SIDE], gram_xy.at[dy * SIDE + dx], at_chip(dy, dx)) for dy, dx in offsets
    ]
    arrive(third_stage)
    third_sum = third_xy[0]
    for i in range(1, chips):
        third_sum = third_sum + third_xy[i]
    third_z[z] = third_sum
    third_last = [send(third_z.at[z], third_z.at[z], at_ring(s)) for s in ring_order(rings)]
    arrive(core_stage)
    core_last = middle_xy(core_c, core_1, core_2)
    arrive(second_stage)
    second_last = middle_xy(second_c, second_1, second_2)

    arrive(gram_stage)
    total = gram_c[chip]
    for i in range(1, chips):
        total = total + gram_xy[i]
    gram_own[...] = total
    gram_ring = [send(gram_own, gram_z.at[s], at_ring(s)) for s in ring_order(rings)]

    arrive(core_last)
    rows_half = core_c.shape[2] // 2
    lane = lax.broadcasted_iota(jnp.int32, (rows_half, 128), 1) // 32
    sums = [
        core_1[0, 0, y] + core_2[0, 0] + core_2[0, 1] + core_2[0, 2],
        core_1[1, 0, x] + core_2[1, 0] + core_2[1, 1] + core_2[1, 2],
    ]
    for group in range(width // 128):
        parts = [sums[k // 2][:, (k % 2) * width + group * 128 : (k % 2) * width + (group + 1) * 128] for k in range(4)]
        for m in range(4):
            piece = None
            for k in range(4):
                shift = (k - m) * 32 % 128
                moved = pltpu.roll(parts[k], shift, 1) if shift else parts[k]
                piece = moved if k == 0 else jnp.where(lane == k, moved, piece)
            pieces[group * 4 + m] = piece
    share_stage = [send(pieces.at[(z + s) % rings], pieces_in.at[s], at_ring(s)) for s in ring_order(rings)]
    arrive(second_last)
    rows_half = second_c.shape[2] // 2
    second_o[0:rows_half, :] = second_prior[0:rows_half, :] + (second_1[0, 0, y] + second_2[0, 0] + second_2[0, 1] + second_2[0, 2])
    second_o[rows_half:, :] = second_prior[rows_half:, :] + (second_1[1, 0, x] + second_2[1, 0] + second_2[1, 1] + second_2[1, 2])

    arrive(gram_ring)
    for i in range(1, rings):
        total = total + gram_z[i]
    gram_done[core, chip] = total
    gram_spread = [send(gram_done.at[core, chip], gram_done.at[core, chip], at_chip(*o)) for o in offsets]
    arrive(gram_spread)
    gram_back = send(gram_done.at[core], gram_done.at[core], partner)
    arrive(share_stage)
    share = pieces[z]
    for i in range(1, rings):
        share = share + pieces_in[i]
    share_o[...] = share
    arrive(third_last)
    third_sum = third_z[0]
    for i in range(1, rings):
        third_sum = third_sum + third_z[i]
    third_o[...] = third_sum
    gram_back.wait_recv()
    gram_o[...] = gram_done[...].reshape(gram_o.shape)
    for copy in send.copies:
        copy.wait_send()


def all_sums(slot_tiles, live_counts, slab, first_t, second_t, third_t, core_f, core_s, first_prior, second_prior):
    vmem, hbm = (pl.BlockSpec(memory_space=m) for m in (pltpu.VMEM, pl.ANY))
    rows, cols, factor, width = first_t.shape[0], second_t.shape[0], first_t.shape[1], core_s.shape[1]
    rings = lax.axis_size("col")
    chips = SIDE * SIDE
    owned, high = second_prior.shape[0], core_f.shape[0] // lax.axis_size("row")
    span = rows // rings
    half = rings // 2

    def f32(*shape):
        return pltpu.VMEM(shape, F32)

    scratch = [
        pltpu.SMEM(slot_tiles.shape, jnp.int32), pltpu.SMEM(live_counts.shape, jnp.int32),
        *(pltpu.VMEM(a.shape, BF16) for a in (slab, first_t, second_t, third_t, core_f, core_s)),
        pltpu.VMEM((2, *second_t.shape), BF16), pltpu.VMEM((rows, 2 * cols), BF16), pltpu.VMEM((rows, 2 * width), BF16),
        f32(rings, span, factor), f32(SIDE, SIDE, 2, owned, factor), f32(SIDE, SIDE, 2, high, 2 * width), f32(1, 2 * factor),
        *(f32(half // 2, span, factor) for _ in range(4)),
        f32(SIDE, SIDE, owned, factor), f32(SIDE, SIDE, high, 2 * width), f32(2, 1, 2 * factor),
        f32(2, SIDE - 1, SIDE, owned // 2, factor), f32(2, SIDE - 1, SIDE, high // 2, 2 * width),
        f32(2, SIDE - 1, owned // 2, factor), f32(2, SIDE - 1, high // 2, 2 * width),
        f32(chips, 1, 2 * factor), f32(rings, 1, 2 * factor),
        f32(2, chips, 8, factor), f32(chips, 8, factor), f32(chips, 8, factor), f32(8, factor), f32(rings, 8, factor),
        f32(2, chips, 8, factor), f32(rings, 8, 128), f32(rings, 8, 128),
        pltpu.SemaphoreType.DMA((16,)), pltpu.SemaphoreType.DMA((160,)), pltpu.SemaphoreType.DMA((160,)),
    ]
    shapes = (first_prior.shape, second_prior.shape, (1, 2 * factor), (factor, factor), (8, 128))
    return pl.pallas_call(
        sums_kernel,
        out_shape=[jax.ShapeDtypeStruct(s, F32) for s in shapes],
        in_specs=[hbm] * 8 + [vmem] * 2,
        out_specs=[vmem] * 5,
        scratch_shapes=scratch,
        compiler_params=pltpu.CompilerParams(collective_id=0, has_side_effects=True, vmem_limit_bytes=60 * 2**20),
    )(slot_tiles, live_counts, slab, first_t, second_t, third_t, core_f, core_s, first_prior, second_prior)


def block_lanes(rows, start, wide):
    shift = start % 128
    value = rows[:, start - shift : start - shift + 128]
    return (pltpu.roll(value, 128 - shift, 1) if shift else value)[:, :wide]


def eliminate(work, reciprocals, size, wide=64, group=16):
    lanes = size // 128

    def across(value):
        return jnp.concatenate([value] * lanes, axis=1)

    for start in range(0, size, wide):
        panel = work[start : start + wide, :]
        finished = []
        inverses = []
        for base in range(0, wide, group):
            high = wide - base
            at = start + base
            row_at = lax.broadcasted_iota(jnp.int32, (high, 128), 0)
            row_low = lax.broadcasted_iota(jnp.int32, (high, size), 0)
            lane_low = lax.broadcasted_iota(jnp.int32, (high, size), 1) - at
            group_row = lax.broadcasted_iota(jnp.int32, (group, 128), 0)
            inverse = jnp.zeros((group, 128), F32)
            columns = [jnp.broadcast_to(panel[:, at + k : at + k + 1], (high, 128)) for k in range(group)]
            taken = jnp.logical_and(lane_low >= 0, lane_low < group)
            panel = jnp.where(taken, jnp.where(lane_low == row_low, 1.0, 0.0), panel)
            for k in range(0, group, 2):
                one, two = columns[k], columns[k + 1]
                a, b, d = one[k : k + 1, :], two[k : k + 1, :], two[k + 1 : k + 2, :]
                inverse_one = 1.0 / a
                inverse_two = a * (1.0 / (a * d - b * b))
                inverse = jnp.where(group_row == k, inverse_one, jnp.where(group_row == k + 1, inverse_two, inverse))
                factor_one = jnp.where(row_at > k, one * inverse_one, 0.0)
                factor_two = jnp.where(row_at > k + 1, (two - factor_one * b) * inverse_two, 0.0)
                for later in range(k + 2, group):
                    value = columns[later] - factor_one * columns[later][k : k + 1, :]
                    columns[later] = value - factor_two * value[k + 1 : k + 2, :]
                panel = panel - across(factor_one) * panel[k : k + 1, :]
                panel = panel - across(factor_two) * panel[k + 1 : k + 2, :]
            finished.append(panel[:group])
            inverses.append(inverse)
            panel = panel[group:]
        panel = jnp.concatenate(finished, axis=0)
        inverse = jnp.concatenate(inverses, axis=0)
        reciprocals[start : start + wide, :] = inverse
        row_full = lax.broadcasted_iota(jnp.int32, (wide, size), 0)
        lane_full = lax.broadcasted_iota(jnp.int32, (wide, size), 1) - start
        panel = jnp.where(lane_full > row_full, jnp.where(lane_full < wide, 0.0, panel), panel)
        work[start : start + wide, :] = panel
        rest = size - start - wide
        if rest:
            inside = jnp.logical_and(lane_full >= 0, lane_full < wide)
            scaled = block_lanes(panel, start, wide) * inverse[:, :wide]
            step = dot(scaled, panel, ((0,), (0,)), HIGHEST)
            for low in range(start + wide, size, wide):
                below = work[low : low + wide, :]
                change = dot(block_lanes(below, start, wide), step, precision=HIGHEST)
                work[low : low + wide, :] = jnp.where(inside, 0.0, below) - change


def inverse_factor(gram, work, reciprocals):
    size = gram.shape[0]
    row = lax.broadcasted_iota(jnp.int32, (size, size), 0)
    lane = lax.broadcasted_iota(jnp.int32, (size, size), 1)
    whole = gram[...]
    diagonal = jnp.where(row == lane, whole, 0.0)
    along = lax.rsqrt(jnp.sum(diagonal, axis=0, keepdims=True))
    work[...] = jnp.where(row == lane, 1.0, whole * along * lax.rsqrt(jnp.sum(diagonal, axis=1, keepdims=True)))
    eliminate(work, reciprocals, size, WIDE, GROUP)
    scale = jnp.concatenate([jnp.sqrt(reciprocals[...])] * (size // 128), axis=1)
    return jnp.where(lane <= row, work[...], 0.0) * scale * along


def basis_kernel(
    gram, sketch, second, third, share, core_t, sketch_o, second_o, third_o, update_o, basis, work, reciprocals, update, sem
):
    turned = share[...].T
    core_rows = core_t[...].astype(F32)
    for p in range(16):
        high, low = divmod(p, 8)
        lower = turned[high * 64 : high * 64 + 32, low : low + 1] * core_rows[0:1, :]
        update[p] = lower + turned[high * 64 + 32 : high * 64 + 64, low : low + 1] * core_rows[1:2, :]
    store = pltpu.make_async_copy(update, update_o, sem)
    store.start()
    factor = third_o.shape[1]
    sketch_o[...] = sketch[...]
    second_o[...] = second[...]
    third_o[0:1, :] = third[:, :factor]
    third_o[1:2, :] = third[:, factor:]
    basis[...] = dot(sketch[...], inverse_factor(gram, work, reciprocals), ((1,), (1,)), HIGHEST)
    store.wait()


def basis_of(gram, sketch, second, third, share, core_t):
    vmem, hbm = pl.BlockSpec(memory_space=pltpu.VMEM), pl.BlockSpec(memory_space=pl.ANY)
    update = (16, 32, core_t.shape[1])
    shapes = (sketch.shape, second.shape, (2, third.shape[1] // 2), update, sketch.shape)
    return pl.pallas_call(
        basis_kernel,
        out_shape=[jax.ShapeDtypeStruct(s, F32) for s in shapes],
        in_specs=[vmem] * 6,
        out_specs=[vmem, vmem, vmem, hbm, vmem],
        scratch_shapes=[
            pltpu.VMEM(gram.shape, F32), pltpu.VMEM((gram.shape[0], 128), F32), pltpu.VMEM(update, F32), pltpu.SemaphoreType.DMA,
        ],
    )(gram, sketch, second, third, share, core_t)


def body(slab, slot_tiles, live_counts, first_prior, second_prior, first_t, second_t, third_t, core_f, core_s, core_t):
    first_sums, second_sums, third_sums, gram, share = all_sums(
        slot_tiles.T, live_counts, slab, first_t, second_t, third_t, core_f, core_s, first_prior, second_prior
    )
    first_sketch, second_sketch, third_sketch, core_update, first_basis = basis_of(
        gram, first_sums, second_sums, third_sums, share, core_t.T
    )
    return (first_sketch, second_sketch, third_sketch, core_update, first_basis)


def solution(mesh):
    both, swapped = P(("row", "col"), None), P(("col", "row"), None)
    return jax.shard_map(
        body,
        mesh=mesh,
        in_specs=(
            P("row", "col"), P("row", "col"), P("row", "col"), both, swapped,
            P("row", None), P("col", None), P(), P(None, "row"), P("col", None), P(),
        ),
        out_specs=(both, swapped, P(), P("row", "col", None), both),
        check_vma=False,
    )
```
